32 devices in a mesh: pb: 8 (over z, y), ka: 4 (over x, core).
Axes of the slice: x: 2, y: 2, z: 4, core: 2. Of those that a mesh axis runs over, the one named last changes fastest.
Arguments:
- query_rows: bfloat16 [4096, 512], P(('pb', 'ka')), may hold values from -8 to 8
- key_rows: bfloat16 [4096, 128], P(('pb', 'ka')), may hold values from -3 to 3
- value_rows: bfloat16 [4096, 128], P(('pb', 'ka')), may hold values from -6 to 6
- outputs: bfloat16 [4096, 512], P(('pb', 'ka')), may hold values from -3 to 3
- out_grads: bfloat16 [4096, 512], P(('pb', 'ka')), may hold values from -6 to 6
- log_totals: float32 [4, 4096], P(None, ('pb', 'ka')), as said below
- selected: int32 [32, 2], P(('pb', 'ka')), may hold values from 0 to 31, as said below
- counts: int32 [32], P(('pb', 'ka')), may hold values from 1 to 2, as said below
Outputs:
- query_grad: float32 [4096, 512], P(('pb', 'ka'))
- key_grad: float32 [4096, 128], P(('pb', 'ka'))
- value_grad: float32 [4096, 128], P(('pb', 'ka'))
The draws below stay inside these ranges and needn't reach their ends.
Inputs may be any that keep to these rules, and one draw needn't show every extreme that they name: log_totals[h, t] is the logarithm of the sum of exp(scores) over all keys that row t of head h attends, with scores and attended keys as in the reference program. `selected`: slot 0 of row q is q itself; the first counts[q] entries of row q are distinct blocks no later than q; entries from slot counts[q] on are padding and are ignored. counts[q] is at most q + 1; the last query block's count is 2.
All inputs are finite; a program needn't handle non-finite values.
Results may differ from the reference program's by a relative error of at most 0.0029.
Values may be sent and summed in bfloat16 or wider, within the bound.
A program may use at most 64 MiB of HBM per device.

```python
import jax
import jax.numpy as jnp
from jax import lax

H = 4
HD = 128
BLK = 128
NB = 32
NSEL = 2


def query_field(key):
    sub_key = jax.random.fold_in(key, 101)
    array_shape = (NB * BLK, H * HD)
    drawn_values = 2.5 * jax.random.truncated_normal(sub_key, -3.2, 3.2, array_shape, jnp.float32)
    return drawn_values.astype(jnp.bfloat16)


def key_field(key):
    sub_key = jax.random.fold_in(key, 202)
    array_shape = (NB * BLK, HD)
    drawn_values = jax.random.truncated_normal(sub_key, -3.0, 3.0, array_shape, jnp.float32)
    return drawn_values.astype(jnp.bfloat16)


def count_field(key):
    sub_key = jax.random.fold_in(key, 303)
    block_index = jnp.arange(NB, dtype=jnp.int32)
    shortfall = jax.random.randint(sub_key, (NB,), 0, NSEL // 2 + 1, dtype=jnp.int32)
    drawn_counts = jnp.minimum(NSEL - shortfall, block_index + 1)
    return jnp.where(block_index == NB - 1, NSEL, drawn_counts).astype(jnp.int32)


def selection_field(key):
    sub_key = jax.random.fold_in(key, 404)
    rows_index = jnp.arange(NB, dtype=jnp.int32)[:, None]
    cols_index = jnp.arange(NB, dtype=jnp.int32)[None, :]
    random_part = jax.random.randint(sub_key, (NB, NB), 0, 131072, dtype=jnp.int32)
    ranking = random_part * NB + cols_index
    ranking = jnp.where(cols_index == rows_index, 131072 * NB + rows_index, ranking)
    ranking = jnp.where(cols_index > rows_index, -1, ranking)
    return lax.top_k(ranking, NSEL)[1].astype(jnp.int32)


def draw_query_rows(key, part):
    return query_field(key)


def draw_key_rows(key, part):
    return key_field(key)


def draw_counts(key, part):
    return count_field(key)


def draw_selected(key, part):
    return selection_field(key)


def draw_log_totals(key, part):
    query_blocks = query_field(key).astype(jnp.float32).reshape(NB, BLK, H, HD)
    key_blocks = key_field(key).astype(jnp.float32).reshape(NB, BLK, HD)
    chosen = selection_field(key)
    valid_counts = count_field(key)
    offsets = jnp.arange(BLK, dtype=jnp.int32)
    slot_index = jnp.arange(NSEL, dtype=jnp.int32)

    def one_block(block_index):
        key_ids = chosen[block_index]
        scores = jnp.einsum('rhd,jcd->hrjc', query_blocks[block_index], key_blocks[key_ids], precision=lax.Precision.HIGHEST) * HD ** (-0.5)
        query_pos = block_index * BLK + offsets
        key_pos = key_ids[:, None] * BLK + offsets[None, :]
        allowed = (slot_index < valid_counts[block_index])[None, :, None] & (key_pos[None, :, :] <= query_pos[:, None, None])
        masked = jnp.where(allowed[None], scores, -1e+30)
        return jax.nn.logsumexp(masked.reshape(H, BLK, NSEL * BLK), axis=2)
    per_block = lax.map(one_block, jnp.arange(NB, dtype=jnp.int32))
    return jnp.transpose(per_block, (1, 0, 2)).reshape(H, NB * BLK).astype(jnp.float32)


def level_of(rng, dims, split, smallest, top_value):
    loudness, own = 1.0, jax.random.fold_in(rng, 6)
    for position, shards_of in split:
        draws = jnp.exp(jax.random.uniform(jax.random.fold_in(own, position), (shards_of,), jnp.float32, smallest / len(split), top_value / len(split)))
        loudness = loudness * jnp.repeat(draws, dims[position] // shards_of).reshape([-1 if axis == position else 1 for axis in range(len(dims))])
    return loudness


def centred(rng, extent, scale, most, split=(), kind=jnp.bfloat16):
    values = scale * jax.random.normal(rng, extent, jnp.float32)
    if split:
        values = values * level_of(rng, extent, split, -0.22, 0.18)
    return jnp.clip(values, -most, most).astype(kind)


def setup_inputs(seed: int = 0) -> dict:
    key_of = jax.random.split(jax.random.key(seed), 9)
    return {
        "query_rows": draw_query_rows(jax.random.fold_in(key_of[8], 71), 0),
        "key_rows": draw_key_rows(jax.random.fold_in(key_of[8], 71), 0),
        "value_rows": centred(key_of[2], (NB * BLK, HD), 1.0, 6.0, ((0, 32),)),
        "outputs": centred(key_of[3], (NB * BLK, H * HD), 0.5, 3.0, ((0, 32),)),
        "out_grads": centred(key_of[4], (NB * BLK, H * HD), 1.0, 6.0, ((0, 32),)),
        "log_totals": draw_log_totals(jax.random.fold_in(key_of[8], 71), 0),
        "selected": draw_selected(jax.random.fold_in(key_of[8], 71), 0),
        "counts": draw_counts(jax.random.fold_in(key_of[8], 71), 0),
    }


HIGHEST_MODE = lax.Precision.HIGHEST


def widen(array_in):
    return array_in.astype(jnp.float32)


def narrow(array_in):
    return lax.optimization_barrier(array_in.astype(jnp.bfloat16)).astype(jnp.float32)


def reference(query_rows, key_rows, value_rows, outputs, out_grads, log_totals, selected, counts):
    seq_rows = NB * BLK
    score_scale = HD ** -0.5
    row_delta = jnp.sum((widen(out_grads) * widen(outputs)).reshape(seq_rows, H, HD), axis=2).T
    key_blocks = key_rows.reshape(NB, BLK, HD)
    value_blocks = value_rows.reshape(NB, BLK, HD)
    slot_index = jnp.arange(NSEL, dtype=jnp.int32)
    offsets = jnp.arange(BLK, dtype=jnp.int32)

    def one_block(key_grads, block_index):
        row_start = block_index * BLK
        key_ids = selected[block_index]
        query_tile = widen(lax.dynamic_slice_in_dim(query_rows, row_start, BLK, 0)).reshape(BLK, H, HD)
        grad_tile = widen(lax.dynamic_slice_in_dim(out_grads, row_start, BLK, 0)).reshape(BLK, H, HD)
        total_tile = lax.dynamic_slice_in_dim(log_totals, row_start, BLK, 1)
        delta_tile = lax.dynamic_slice_in_dim(row_delta, row_start, BLK, 1)
        key_sel = widen(key_blocks[key_ids])
        value_sel = widen(value_blocks[key_ids])
        scores = jnp.einsum("rhd,jcd->hrjc", query_tile, key_sel, precision=HIGHEST_MODE) * score_scale
        query_pos = row_start + offsets
        key_pos = key_ids[:, None] * BLK + offsets[None, :]
        allowed = (slot_index < counts[block_index])[None, :, None] & (key_pos[None, :, :] <= query_pos[:, None, None])
        probs = jnp.exp(jnp.where(allowed[None], scores - total_tile[:, :, None, None], -1e30))
        prob_grads = jnp.einsum("rhd,jcd->hrjc", grad_tile, value_sel, precision=HIGHEST_MODE)
        score_grads = probs * (prob_grads - delta_tile[:, :, None, None])
        rounded_probs = narrow(probs)
        rounded_grads = narrow(score_grads)
        query_part = jnp.einsum("hrjc,jcd->rhd", rounded_grads, key_sel, precision=HIGHEST_MODE) * score_scale
        key_part = jnp.einsum("hrjc,rhd->jcd", rounded_grads, query_tile, precision=HIGHEST_MODE) * score_scale
        value_part = jnp.einsum("hrjc,rhd->jcd", rounded_probs, grad_tile, precision=HIGHEST_MODE)
        key_grads = key_grads.at[key_ids].add(jnp.concatenate([key_part, value_part], 2))
        return key_grads, query_part.reshape(BLK, H * HD)

    start_grads = jnp.zeros((NB, BLK, 2 * HD), jnp.float32)
    key_grads, query_grad = lax.scan(one_block, start_grads, jnp.arange(NB, dtype=jnp.int32))
    query_grad = query_grad.reshape(seq_rows, H * HD)
    key_grads = key_grads.reshape(seq_rows, 2 * HD)
    return query_grad, key_grads[:, :HD], key_grads[:, HD:]
```

```python
import functools

import jax
import jax.numpy as jnp
from jax import lax
from jax.experimental import pallas as pl
from jax.experimental.pallas import tpu as pltpu
from jax.sharding import PartitionSpec as P

VERY_LOW = -1e30


def passed_along(value, axis, steps):
    count = lax.axis_size(axis)
    pairs = [(source, (source + steps) % count) for source in range(count)]
    return lax.ppermute(value, axis, pairs)


def head_sums(grad_rows, out_rows, head_width):
    row_total = grad_rows.shape[0]
    part_heads = grad_rows.shape[1] // head_width
    product = grad_rows.astype(jnp.float32) * out_rows.astype(jnp.float32)
    return jnp.sum(product.reshape(row_total, part_heads, head_width), axis=2).T


def shards(query_rows, key_rows, value_rows, outputs, out_grads, log_totals, selected, counts):
    ka_count = lax.axis_size("ka")
    ka_index = lax.axis_index("ka")
    pb_index = lax.axis_index("pb")
    block_count = selected.shape[0]
    slot_count = selected.shape[1]
    head_width = key_rows.shape[1]
    block_rows = query_rows.shape[0] // block_count
    score_scale = head_width ** (-0.5)
    key_pairs = jnp.concatenate([key_rows, value_rows], 1)
    column_keys = lax.all_gather(key_pairs, "pb", axis=0, tiled=True)
    peer_slots, peer_counts = (
        lax.all_gather(selected, "ka", axis=0, tiled=True),
        lax.all_gather(counts, "ka", axis=0, tiled=True),
    )
    key_grads = jnp.zeros((column_keys.shape[0], 2 * head_width), jnp.float32)
    row_offsets = jnp.arange(block_rows, dtype=jnp.int32)
    flat_owner = jnp.repeat(jnp.arange(block_count, dtype=jnp.int32), slot_count)
    flat_slot = jnp.tile(jnp.arange(slot_count, dtype=jnp.int32), block_count)
    flat_places = jnp.arange(block_count * slot_count, dtype=jnp.int32)

    def visit_block(row_stack, query_grad, stat_stack, anchor, key_grads):
        held_query = row_stack[0]
        held_grad = row_stack[1]
        total_rows = stat_stack[0]
        delta_rows = head_sums(row_stack[1], row_stack[2], head_width)
        part_heads = total_rows.shape[0]
        held_slots = lax.dynamic_slice_in_dim(
            peer_slots, anchor * block_count, block_count, 0
        ).reshape(-1)
        held_counts = jnp.repeat(
            lax.dynamic_slice_in_dim(peer_counts, anchor * block_count, block_count, 0), slot_count
        )
        first_block = (pb_index * ka_count + anchor) * block_count
        wanted = (flat_slot < held_counts) & (held_slots // block_count % ka_count == ka_index)
        position = jnp.cumsum(wanted.astype(jnp.int32)) - 1
        placed = wanted[:, None] & (position[:, None] == flat_places[None, :])
        packed_ids = jnp.sum(jnp.where(placed, held_slots[:, None], 0), axis=0)
        packed_owner = jnp.sum(jnp.where(placed, flat_owner[:, None], 0), axis=0)
        live_tiles = jnp.sum(wanted.astype(jnp.int32))

        def one_tile(tile_index, loop_state):
            query_grad, key_grads = loop_state
            key_block = packed_ids[tile_index]
            owner_block = packed_owner[tile_index]
            key_start = (
                key_block // (block_count * ka_count) * block_count + key_block % block_count
            ) * block_rows
            pair_tile = lax.dynamic_slice_in_dim(column_keys, key_start, block_rows, 0)
            key_tile = pair_tile[:, :head_width]
            value_tile = pair_tile[:, head_width:]
            query_tile = held_query.reshape(block_rows, part_heads, head_width)
            grad_tile = held_grad.reshape(block_rows, part_heads, head_width)
            scores = (
                jnp.einsum("rhd,cd->hrc", query_tile, key_tile, preferred_element_type=jnp.float32)
                * score_scale
            )
            query_pos = (first_block + owner_block) * block_rows + row_offsets
            key_pos = key_block * block_rows + row_offsets
            allowed = key_pos[None, :] <= query_pos[:, None]
            probs_full = jnp.exp(
                jnp.where(allowed[None], scores - total_rows[:, :, None], VERY_LOW)
            )
            prob_grads = jnp.einsum(
                "rhd,cd->hrc", grad_tile, value_tile, preferred_element_type=jnp.float32
            )
            score_grads = probs_full * (prob_grads - delta_rows[:, :, None])
            rounded_probs = probs_full.astype(jnp.bfloat16)
            rounded_grads = score_grads.astype(jnp.bfloat16)
            value_part = jnp.einsum(
                "hrc,rhd->cd", rounded_probs, grad_tile, preferred_element_type=jnp.float32
            )
            key_part = (
                jnp.einsum(
                    "hrc,rhd->cd", rounded_grads, query_tile, preferred_element_type=jnp.float32
                )
                * score_scale
            )
            query_part = (
                jnp.einsum(
                    "hrc,cd->rhd", rounded_grads, key_tile, preferred_element_type=jnp.float32
                )
                * score_scale
            )
            old_query = query_grad
            query_grad = old_query + query_part.reshape(block_rows, -1)
            old_keys = lax.dynamic_slice_in_dim(key_grads, key_start, block_rows, 0)
            key_grads = lax.dynamic_update_slice_in_dim(
                key_grads, old_keys + jnp.concatenate([key_part, value_part], 1), key_start, 0
            )
            return (query_grad, key_grads)

        return lax.fori_loop(0, live_tiles, one_tile, (query_grad, key_grads))

    query_part = query_rows
    grad_zero = jnp.zeros(query_part.shape, jnp.float32)
    row_stack = jnp.stack([query_part, out_grads, outputs])
    query_grad = grad_zero
    stat_stack = log_totals[None]

    def forward_hop(hop_index, loop_state):
        row_stack, query_grad, stat_stack, key_grads = loop_state
        anchor = (ka_index - hop_index) % ka_count
        query_grad, key_grads = visit_block(row_stack, query_grad, stat_stack, anchor, key_grads)
        row_stack = passed_along(row_stack, "ka", 1)
        query_grad, stat_stack = passed_along((query_grad, stat_stack), "ka", 1)
        return (row_stack, query_grad, stat_stack, key_grads)

    row_stack, query_grad, stat_stack, key_grads = lax.fori_loop(
        0, ka_count - 1, forward_hop, (row_stack, query_grad, stat_stack, key_grads)
    )
    query_grad, key_grads = visit_block(
        row_stack, query_grad, stat_stack, (ka_index + 1) % ka_count, key_grads
    )
    query_grad = passed_along(query_grad, "ka", 1)
    owned_grads = lax.psum_scatter(key_grads, "pb", scatter_dimension=0, tiled=True)
    return (query_grad, owned_grads[:, :head_width], owned_grads[:, head_width:])


MESH = pl.DeviceIdType.MESH
VMEM_BUDGET = 40 << 20


def tile_grads(key_tile, value_tile, query_stack, grad_stack, total_row, delta_row, allowed, scale):
    nt = (((1,), (1,)), ((), ()))
    scores = lax.dot_general(key_tile, query_stack, nt, preferred_element_type=jnp.float32) * scale
    probs = jnp.exp(jnp.where(allowed, scores - total_row, VERY_LOW))
    prob_grads = lax.dot_general(value_tile, grad_stack, nt, preferred_element_type=jnp.float32)
    score_grads = (probs * (prob_grads - delta_row)).astype(jnp.bfloat16)
    value_part = jnp.dot(probs.astype(jnp.bfloat16), grad_stack, preferred_element_type=jnp.float32)
    key_part = jnp.dot(score_grads, query_stack, preferred_element_type=jnp.float32) * scale
    query_part = (
        lax.dot_general(
            score_grads, key_tile, (((0,), (0,)), ((), ())), preferred_element_type=jnp.float32
        )
        * scale
    )
    return query_part, key_part, value_part


def whole_kernel(
    ka_count, inner, line_count, extra,
    query_ref, key_ref, value_ref, out_ref, grad_ref, total_ref, selected_ref, counts_ref,
    query_grad_ref, key_grad_ref, value_grad_ref,
    plane_kv, line_kv, line_kv_out, plane_part, line_part, line_part_out,
    plane_info, line_info, query_stack, grad_stack, query_acc, key_acc, value_acc,
    info_send_p, info_recv_p, info_send_l, info_recv_l,
    kv_send_p, kv_recv_p, kv_send_l, kv_recv_l,
    part_send_p, part_recv_p, part_send_l, part_recv_l, load_sem,
):
    plane_count = inner * ka_count
    pb_index, ka_index = lax.axis_index("pb"), lax.axis_index("ka")
    line = lax.div(pb_index, inner)
    row = lax.rem(pb_index, inner)
    place = row * ka_count + ka_index
    block_rows, head_width = key_ref.shape
    heads = total_ref.shape[0]
    scale = head_width ** (-0.5)
    block = line * plane_count + place

    loads = [
        pltpu.make_async_copy(key_ref, plane_kv.at[place, pl.ds(0, block_rows)], load_sem.at[0]),
        pltpu.make_async_copy(value_ref, plane_kv.at[place, pl.ds(block_rows, block_rows)], load_sem.at[1]),
    ]
    for load in loads:
        load.start()

    def plane_peer(offset):
        peer = lax.rem(place + offset, plane_count)
        return peer, (line * inner + lax.div(peer, ka_count), lax.rem(peer, ka_count))

    def line_peer(offset):
        peer = lax.rem(line + offset, line_count)
        return peer, (peer * inner + row, ka_index)

    barrier = pltpu.get_barrier_semaphore()
    for offset in range(1, plane_count):
        pl.semaphore_signal(barrier, inc=1, device_id=plane_peer(offset)[1], device_id_type=MESH)
    for offset in range(1, line_count):
        pl.semaphore_signal(barrier, inc=1, device_id=line_peer(offset)[1], device_id_type=MESH)

    targets = [
        jnp.where(slot + 1 < counts_ref[0], selected_ref[0, slot + 1], -1) for slot in range(extra)
    ]
    for slot in range(extra):
        lines = jnp.full((8, 128), targets[slot], jnp.int32)
        plane_info[place, slot] = lines
        line_info[line, slot] = lines
    for load in loads:
        load.wait()
    pl.semaphore_wait(barrier, plane_count + line_count - 2)

    def exchange(peer_of, count, me, source_of, target, send, recv):
        copies = []
        for offset in range(1, count):
            peer, device = peer_of(offset)
            copy = pltpu.make_async_remote_copy(
                src_ref=source_of(peer), dst_ref=target.at[me], send_sem=send.at[offset],
                recv_sem=recv.at[me], device_id=device, device_id_type=MESH,
            )
            copy.start()
            copies.append(copy)
        return copies

    def arrive(peer_of, count, target, send, recv):
        for offset in range(1, count):
            peer, device = peer_of(offset)
            pltpu.make_async_remote_copy(
                src_ref=target.at[peer], dst_ref=target.at[peer], send_sem=send.at[offset],
                recv_sem=recv.at[peer], device_id=device, device_id_type=MESH,
            ).wait_recv()

    sent = []
    sent += exchange(line_peer, line_count, line, lambda p: line_info.at[line], line_info, info_send_l, info_recv_l)
    sent += exchange(plane_peer, plane_count, place, lambda p: plane_info.at[place], plane_info, info_send_p, info_recv_p)
    sent += exchange(plane_peer, plane_count, place, lambda p: plane_kv.at[place], plane_kv, kv_send_p, kv_recv_p)

    deltas = []
    for head in range(heads):
        columns = pl.ds(head * head_width, head_width)
        rows = pl.ds(head * block_rows, block_rows)
        query_stack[rows, :] = query_ref[:, columns]
        grad_stack[rows, :] = grad_ref[:, columns]
        product = grad_ref[:, columns].astype(jnp.float32) * out_ref[:, columns].astype(jnp.float32)
        deltas.append(jnp.sum(product.T, axis=0, keepdims=True))
    delta_row = jnp.concatenate(deltas, axis=1)
    total_row = jnp.concatenate([total_ref[head : head + 1, :] for head in range(heads)], axis=1)
    stack_shape = (block_rows, heads * block_rows)
    key_offset = lax.broadcasted_iota(jnp.int32, stack_shape, 0)
    query_offset = lax.rem(lax.broadcasted_iota(jnp.int32, stack_shape, 1), block_rows)

    arrive(line_peer, line_count, line_info, info_send_l, info_recv_l)
    arrive(plane_peer, plane_count, plane_info, info_send_p, info_recv_p)
    arrive(plane_peer, plane_count, plane_kv, kv_send_p, kv_recv_p)

    for offset in range(line_count):
        peer, _ = line_peer(offset)
        for slot in range(extra):
            wanted = line_info[peer, slot][0:1, :]
            picked = jnp.zeros(plane_kv.shape[1:], jnp.float32)
            for other in range(plane_count):
                picked = jnp.where(
                    wanted == line * plane_count + other, plane_kv[other].astype(jnp.float32), picked
                )
            if offset == 0:
                line_kv[line, slot] = picked.astype(jnp.bfloat16)
            else:
                line_kv_out[peer, slot] = picked.astype(jnp.bfloat16)
    sent += exchange(line_peer, line_count, line, lambda p: line_kv_out.at[p], line_kv, kv_send_l, kv_recv_l)

    query_part, key_part, value_part = tile_grads(
        key_ref[...], value_ref[...], query_stack[...], grad_stack[...], total_row, delta_row,
        key_offset <= query_offset, scale,
    )
    query_acc[...] = query_part
    key_acc[...] = key_part
    value_acc[...] = value_part

    arrive(line_peer, line_count, line_kv, kv_send_l, kv_recv_l)
    for slot in range(extra):
        source = lax.div(jnp.maximum(targets[slot], 0), plane_count)
        pair = line_kv[source, slot]
        allowed = (key_offset + targets[slot] * block_rows <= query_offset + block * block_rows) & (
            jnp.full(stack_shape, targets[slot], jnp.int32) >= 0
        )
        query_part, key_part, value_part = tile_grads(
            pair[:block_rows], pair[block_rows:], query_stack[...], grad_stack[...], total_row,
            delta_row, allowed, scale,
        )
        query_acc[...] += query_part
        plane_part[place, slot, :block_rows] = key_part.astype(jnp.bfloat16)
        plane_part[place, slot, block_rows:] = value_part.astype(jnp.bfloat16)
    sent += exchange(plane_peer, plane_count, place, lambda p: plane_part.at[place], plane_part, part_send_p, part_recv_p)
    for head in range(heads):
        query_grad_ref[:, pl.ds(head * head_width, head_width)] = query_acc[
            pl.ds(head * block_rows, block_rows), :
        ]
    arrive(plane_peer, plane_count, plane_part, part_send_p, part_recv_p)

    sums = jnp.zeros(plane_part.shape[2:], jnp.float32)
    for offset in range(line_count - 1, -1, -1):
        peer, _ = line_peer(offset)
        sums = jnp.zeros(plane_part.shape[2:], jnp.float32)
        for other in range(plane_count):
            for slot in range(extra):
                aimed = plane_info[other, slot][0:1, :] == peer * plane_count + place
                sums = sums + jnp.where(aimed, plane_part[other, slot].astype(jnp.float32), 0.0)
        if offset:
            line_part_out[peer] = sums.astype(jnp.bfloat16)
    sent += exchange(line_peer, line_count, line, lambda p: line_part_out.at[p], line_part, part_send_l, part_recv_l)
    key_total = key_acc[...] + sums[:block_rows]
    value_total = value_acc[...] + sums[block_rows:]
    arrive(line_peer, line_count, line_part, part_send_l, part_recv_l)
    for offset in range(1, line_count):
        peer, _ = line_peer(offset)
        pair = line_part[peer].astype(jnp.float32)
        key_total = key_total + pair[:block_rows]
        value_total = value_total + pair[block_rows:]
    key_grad_ref[...] = key_total
    value_grad_ref[...] = value_total
    for copy in sent:
        copy.wait_send()


def kernel_shards(query_rows, key_rows, value_rows, outputs, out_grads, log_totals, selected, counts):
    ka_count, pb_count = lax.axis_size("ka"), lax.axis_size("pb")
    inner = 2 if pb_count % 2 == 0 else 1
    line_count, plane_count = pb_count // inner, inner * ka_count
    extra = selected.shape[1] - 1
    block_rows, head_width = key_rows.shape
    heads = log_totals.shape[0]
    pair = (2 * block_rows, head_width)
    dma = pltpu.SemaphoreType.DMA
    vmem = pl.BlockSpec(memory_space=pltpu.VMEM)
    smem = pl.BlockSpec(memory_space=pltpu.SMEM)
    bf, f32 = jnp.bfloat16, jnp.float32
    return pl.pallas_call(
        functools.partial(whole_kernel, ka_count, inner, line_count, extra),
        out_shape=(
            jax.ShapeDtypeStruct(query_rows.shape, f32),
            jax.ShapeDtypeStruct(key_rows.shape, f32),
            jax.ShapeDtypeStruct(key_rows.shape, f32),
        ),
        in_specs=[vmem] * 6 + [smem] * 2,
        out_specs=(vmem, vmem, vmem),
        scratch_shapes=[
            pltpu.VMEM((plane_count, *pair), bf),
            pltpu.VMEM((line_count, extra, *pair), bf),
            pltpu.VMEM((line_count, extra, *pair), bf),
            pltpu.VMEM((plane_count, extra, *pair), bf),
            pltpu.VMEM((line_count, *pair), bf),
            pltpu.VMEM((line_count, *pair), bf),
            pltpu.VMEM((plane_count, extra, 8, 128), jnp.int32),
            pltpu.VMEM((line_count, extra, 8, 128), jnp.int32),
            pltpu.VMEM((heads * block_rows, head_width), bf),
            pltpu.VMEM((heads * block_rows, head_width), bf),
            pltpu.VMEM((heads * block_rows, head_width), f32),
            pltpu.VMEM((block_rows, head_width), f32),
            pltpu.VMEM((block_rows, head_width), f32),
            *[dma((count,)) for count in (plane_count, plane_count, line_count, line_count) * 3],
            dma((2,)),
        ],
        compiler_params=pltpu.CompilerParams(collective_id=0, has_side_effects=True),
    )(query_rows, key_rows, value_rows, outputs, out_grads, log_totals, selected, counts)


def fits_kernel(query_rows, key_rows, value_rows, outputs, out_grads, log_totals, selected, counts):
    pb_count, ka_count = lax.axis_size("pb"), lax.axis_size("ka")
    block_rows, head_width = key_rows.shape
    inner = 2 if pb_count % 2 == 0 else 1
    extra = selected.shape[1] - 1
    tile_bytes = 4 * block_rows * head_width
    tiles = (pb_count // inner) * (2 * extra + 2) + inner * ka_count * (1 + extra)
    return (
        selected.shape[0] == 1
        and extra > 0
        and block_rows == head_width == 128
        and tiles * tile_bytes < VMEM_BUDGET
    )


def either(*arrays):
    return kernel_shards(*arrays) if fits_kernel(*arrays) else shards(*arrays)


def solution(mesh):
    return jax.shard_map(
        either,
        mesh=mesh,
        in_specs=(
            P(("pb", "ka"), None),
            P(("pb", "ka"), None),
            P(("pb", "ka"), None),
            P(("pb", "ka"), None),
            P(("pb", "ka"), None),
            P(None, ("pb", "ka")),
            P(("pb", "ka"), None),
            P(("pb", "ka")),
        ),
        out_specs=(P(("pb", "ka"), None), P(("pb", "ka"), None), P(("pb", "ka"), None)),
        check_vma=False,
    )
```

```python
import functools

import jax
import jax.numpy as jnp
from jax import lax
from jax.experimental import pallas as pl
from jax.experimental.pallas import tpu as pltpu
from jax.sharding import PartitionSpec as P

VERY_LOW = -1e30


def passed_along(value, axis, steps):
    count = lax.axis_size(axis)
    pairs = [(source, (source + steps) % count) for source in range(count)]
    return lax.ppermute(value, axis, pairs)


def head_sums(grad_rows, out_rows, head_width):
    row_total = grad_rows.shape[0]
    part_heads = grad_rows.shape[1] // head_width
    product = grad_rows.astype(jnp.float32) * out_rows.astype(jnp.float32)
    return jnp.sum(product.reshape(row_total, part_heads, head_width), axis=2).T


def shards(query_rows, key_rows, value_rows, outputs, out_grads, log_totals, selected, counts):
    ka_count = lax.axis_size("ka")
    ka_index = lax.axis_index("ka")
    pb_index = lax.axis_index("pb")
    block_count = selected.shape[0]
    slot_count = selected.shape[1]
    head_width = key_rows.shape[1]
    block_rows = query_rows.shape[0] // block_count
    score_scale = head_width ** (-0.5)
    key_pairs = jnp.concatenate([key_rows, value_rows], 1)
    column_keys = lax.all_gather(key_pairs, "pb", axis=0, tiled=True)
    peer_slots, peer_counts = (
        lax.all_gather(selected, "ka", axis=0, tiled=True),
        lax.all_gather(counts, "ka", axis=0, tiled=True),
    )
    key_grads = jnp.zeros((column_keys.shape[0], 2 * head_width), jnp.float32)
    row_offsets = jnp.arange(block_rows, dtype=jnp.int32)
    flat_owner = jnp.repeat(jnp.arange(block_count, dtype=jnp.int32), slot_count)
    flat_slot = jnp.tile(jnp.arange(slot_count, dtype=jnp.int32), block_count)
    flat_places = jnp.arange(block_count * slot_count, dtype=jnp.int32)

    def visit_block(row_stack, query_grad, stat_stack, anchor, key_grads):
        held_query = row_stack[0]
        held_grad = row_stack[1]
        total_rows = stat_stack[0]
        delta_rows = head_sums(row_stack[1], row_stack[2], head_width)
        part_heads = total_rows.shape[0]
        held_slots = lax.dynamic_slice_in_dim(
            peer_slots, anchor * block_count, block_count, 0
        ).reshape(-1)
        held_counts = jnp.repeat(
            lax.dynamic_slice_in_dim(peer_counts, anchor * block_count, block_count, 0), slot_count
        )
        first_block = (pb_index * ka_count + anchor) * block_count
        wanted = (flat_slot < held_counts) & (held_slots // block_count % ka_count == ka_index)
        position = jnp.cumsum(wanted.astype(jnp.int32)) - 1
        placed = wanted[:, None] & (position[:, None] == flat_places[None, :])
        packed_ids = jnp.sum(jnp.where(placed, held_slots[:, None], 0), axis=0)
        packed_owner = jnp.sum(jnp.where(placed, flat_owner[:, None], 0), axis=0)
        live_tiles = jnp.sum(wanted.astype(jnp.int32))

        def one_tile(tile_index, loop_state):
            query_grad, key_grads = loop_state
            key_block = packed_ids[tile_index]
            owner_block = packed_owner[tile_index]
            key_start = (
                key_block // (block_count * ka_count) * block_count + key_block % block_count
            ) * block_rows
            pair_tile = lax.dynamic_slice_in_dim(column_keys, key_start, block_rows, 0)
            key_tile = pair_tile[:, :head_width]
            value_tile = pair_tile[:, head_width:]
            query_tile = held_query.reshape(block_rows, part_heads, head_width)
            grad_tile = held_grad.reshape(block_rows, part_heads, head_width)
            scores = (
                jnp.einsum("rhd,cd->hrc", query_tile, key_tile, preferred_element_type=jnp.float32)
                * score_scale
            )
            query_pos = (first_block + owner_block) * block_rows + row_offsets
            key_pos = key_block * block_rows + row_offsets
            allowed = key_pos[None, :] <= query_pos[:, None]
            probs_full = jnp.exp(
                jnp.where(allowed[None], scores - total_rows[:, :, None], VERY_LOW)
            )
            prob_grads = jnp.einsum(
                "rhd,cd->hrc", grad_tile, value_tile, preferred_element_type=jnp.float32
            )
            score_grads = probs_full * (prob_grads - delta_rows[:, :, None])
            rounded_probs = probs_full.astype(jnp.bfloat16)
            rounded_grads = score_grads.astype(jnp.bfloat16)
            value_part = jnp.einsum(
                "hrc,rhd->cd", rounded_probs, grad_tile, preferred_element_type=jnp.float32
            )
            key_part = (
                jnp.einsum(
                    "hrc,rhd->cd", rounded_grads, query_tile, preferred_element_type=jnp.float32
                )
                * score_scale
            )
            query_part = (
                jnp.einsum(
                    "hrc,cd->rhd", rounded_grads, key_tile, preferred_element_type=jnp.float32
                )
                * score_scale
            )
            old_query = query_grad
            query_grad = old_query + query_part.reshape(block_rows, -1)
            old_keys = lax.dynamic_slice_in_dim(key_grads, key_start, block_rows, 0)
            key_grads = lax.dynamic_update_slice_in_dim(
                key_grads, old_keys + jnp.concatenate([key_part, value_part], 1), key_start, 0
            )
            return (query_grad, key_grads)

        return lax.fori_loop(0, live_tiles, one_tile, (query_grad, key_grads))

    query_part = query_rows
    grad_zero = jnp.zeros(query_part.shape, jnp.float32)
    row_stack = jnp.stack([query_part, out_grads, outputs])
    query_grad = grad_zero
    stat_stack = log_totals[None]

    def forward_hop(hop_index, loop_state):
        row_stack, query_grad, stat_stack, key_grads = loop_state
        anchor = (ka_index - hop_index) % ka_count
        query_grad, key_grads = visit_block(row_stack, query_grad, stat_stack, anchor, key_grads)
        row_stack = passed_along(row_stack, "ka", 1)
        query_grad, stat_stack = passed_along((query_grad, stat_stack), "ka", 1)
        return (row_stack, query_grad, stat_stack, key_grads)

    row_stack, query_grad, stat_stack, key_grads = lax.fori_loop(
        0, ka_count - 1, forward_hop, (row_stack, query_grad, stat_stack, key_grads)
    )
    query_grad, key_grads = visit_block(
        row_stack, query_grad, stat_stack, (ka_index + 1) % ka_count, key_grads
    )
    query_grad = passed_along(query_grad, "ka", 1)
    owned_grads = lax.psum_scatter(key_grads, "pb", scatter_dimension=0, tiled=True)
    return (query_grad, owned_grads[:, :head_width], owned_grads[:, head_width:])


MESH = pl.DeviceIdType.MESH
VMEM_BUDGET = 40 << 20


def tile_weights(key_tile, value_tile, query_stack, grad_stack, total_row, delta_row, allowed, scale):
    nt = (((1,), (1,)), ((), ()))
    scores = lax.dot_general(key_tile, query_stack, nt, preferred_element_type=jnp.float32) * scale
    probs = jnp.exp(jnp.where(allowed, scores - total_row, VERY_LOW))
    prob_grads = lax.dot_general(value_tile, grad_stack, nt, preferred_element_type=jnp.float32)
    score_grads = probs * (prob_grads - delta_row)
    return probs.astype(jnp.bfloat16), score_grads.astype(jnp.bfloat16)


def query_share(score_grads, key_tile, scale):
    tn = (((0,), (0,)), ((), ()))
    return lax.dot_general(score_grads, key_tile, tn, preferred_element_type=jnp.float32) * scale


def whole_kernel(
    ka_count, inner, line_count, extra,
    query_hbm, key_hbm, value_hbm, out_hbm, grad_hbm, total_hbm, selected_ref, counts_ref,
    query_grad_hbm, key_grad_ref, value_grad_ref,
    query_ref, out_ref, grad_ref, total_ref,
    key_plane, key_line, key_line_out, value_line, value_plane, value_plane_out,
    kgrad_plane, kgrad_line, kgrad_line_out, vgrad_line, vgrad_plane, vgrad_plane_out,
    plane_info, line_info, query_stack, grad_stack, query_acc, key_acc, value_acc,
    info_send_p, info_recv_p, info_send_l, info_recv_l,
    key_send_p, key_recv_p, key_send_l, key_recv_l,
    value_send_p, value_recv_p, value_send_l, value_recv_l,
    kgrad_send_p, kgrad_recv_p, kgrad_send_l, kgrad_recv_l,
    vgrad_send_p, vgrad_recv_p, vgrad_send_l, vgrad_recv_l,
    load_sem,
):
    bf, f32 = jnp.bfloat16, jnp.float32
    plane_count = inner * ka_count
    pb_index, ka_index = lax.axis_index("pb"), lax.axis_index("ka")
    line = lax.div(pb_index, inner)
    row = lax.rem(pb_index, inner)
    place = row * ka_count + ka_index
    block_rows, head_width = key_hbm.shape
    heads = total_hbm.shape[0]
    scale = head_width ** (-0.5)
    block = line * plane_count + place

    def plane_peer(offset):
        peer = lax.rem(place + offset, plane_count)
        return peer, (line * inner + lax.div(peer, ka_count), lax.rem(peer, ka_count))

    def line_peer(offset):
        peer = lax.rem(line + offset, line_count)
        return peer, (peer * inner + row, ka_index)

    plane = (plane_peer, plane_count, place)
    column = (line_peer, line_count, line)

    barrier = pltpu.get_barrier_semaphore()
    for peer_of, count, _ in (plane, column):
        for offset in range(1, count):
            pl.semaphore_signal(barrier, inc=1, device_id=peer_of(offset)[1], device_id_type=MESH)
    loads = [
        pltpu.make_async_copy(source, target, load_sem.at[index])
        for index, (source, target) in enumerate((
            (key_hbm, key_plane.at[place]), (value_hbm, value_line.at[line]),
            (query_hbm, query_ref), (grad_hbm, grad_ref), (out_hbm, out_ref), (total_hbm, total_ref),
        ))
    ]
    for load in loads:
        load.start()

    targets = [
        jnp.where(slot + 1 < counts_ref[0], selected_ref[0, slot + 1], -1) for slot in range(extra)
    ]
    for slot in range(extra):
        lines = jnp.full((8, 128), targets[slot], jnp.int32)
        plane_info[place, slot] = lines
        line_info[line, slot] = lines

    sent = []

    def send(group, offset, source, target, send_sem, recv_sem):
        peer_of, _, me = group
        copy = pltpu.make_async_remote_copy(
            src_ref=source, dst_ref=target.at[me], send_sem=send_sem.at[offset],
            recv_sem=recv_sem.at[me], device_id=peer_of(offset)[1], device_id_type=MESH,
        )
        copy.start()
        sent.append(copy)

    def spread(group, target, send_sem, recv_sem):
        for offset in range(1, group[1]):
            send(group, offset, target.at[group[2]], target, send_sem, recv_sem)

    def arrive(group, target, send_sem, recv_sem):
        peer_of, count, _ = group
        for offset in range(1, count):
            peer, device = peer_of(offset)
            pltpu.make_async_remote_copy(
                src_ref=target.at[peer], dst_ref=target.at[peer], send_sem=send_sem.at[offset],
                recv_sem=recv_sem.at[peer], device_id=device, device_id_type=MESH,
            ).wait_recv()

    loads[0].wait()
    loads[1].wait()
    pl.semaphore_wait(barrier, plane_count + line_count - 2)
    spread(column, line_info, info_send_l, info_recv_l)
    spread(plane, plane_info, info_send_p, info_recv_p)
    spread(column, value_line, value_send_l, value_recv_l)
    spread(plane, key_plane, key_send_p, key_recv_p)

    for load in loads[2:]:
        load.wait()
    deltas = []
    for head in range(heads):
        columns = pl.ds(head * head_width, head_width)
        rows = pl.ds(head * block_rows, block_rows)
        query_stack[rows, :] = query_ref[:, columns]
        grad_stack[rows, :] = grad_ref[:, columns]
        product = grad_ref[:, columns].astype(f32) * out_ref[:, columns].astype(f32)
        deltas.append(jnp.sum(product.T, axis=0, keepdims=True))
    delta_row = jnp.concatenate(deltas, axis=1)
    total_row = jnp.concatenate([total_ref[head : head + 1, :] for head in range(heads)], axis=1)
    stack_shape = (block_rows, heads * block_rows)
    key_offset = lax.broadcasted_iota(jnp.int32, stack_shape, 0)
    query_offset = lax.rem(lax.broadcasted_iota(jnp.int32, stack_shape, 1), block_rows)

    arrive(column, line_info, info_send_l, info_recv_l)
    arrive(plane, plane_info, info_send_p, info_recv_p)

    def pick(group, info, held, held_count, first, step, out, target, send_sem, recv_sem):
        peer_of, count, me = group
        for offset in list(range(1, count)) + [0]:
            peer, _ = peer_of(offset)
            for slot in range(extra):
                wanted = info[peer, slot][0:1, :]
                picked = jnp.zeros(held.shape[1:], f32)
                for other in range(held_count):
                    picked = jnp.where(wanted == first + other * step, held[other].astype(f32), picked)
                if offset:
                    out[peer, slot] = picked.astype(bf)
                else:
                    target[me, slot] = picked.astype(bf)
            if offset:
                send(group, offset, out.at[peer], target, send_sem, recv_sem)

    arrive(column, value_line, value_send_l, value_recv_l)
    pick(plane, plane_info, value_line, line_count, place, plane_count,
         value_plane_out, value_plane, value_send_p, value_recv_p)
    arrive(plane, key_plane, key_send_p, key_recv_p)
    pick(column, line_info, key_plane, plane_count, line * plane_count, 1,
         key_line_out, key_line, key_send_l, key_recv_l)

    own_key = key_plane[place]
    probs, score_grads = tile_weights(
        own_key, value_line[line], query_stack[...], grad_stack[...], total_row, delta_row,
        key_offset <= query_offset, scale,
    )
    query_acc[...] = query_share(score_grads, own_key, scale)
    key_acc[...] = jnp.dot(score_grads, query_stack[...], preferred_element_type=f32) * scale
    value_acc[...] = jnp.dot(probs, grad_stack[...], preferred_element_type=f32)

    arrive(column, key_line, key_send_l, key_recv_l)
    arrive(plane, value_plane, value_send_p, value_recv_p)
    late = []
    for slot in range(extra):
        listed = jnp.maximum(targets[slot], 0)
        key_tile = key_line[lax.div(listed, plane_count), slot]
        value_tile = value_plane[lax.rem(listed, plane_count), slot]
        allowed = (key_offset + targets[slot] * block_rows <= query_offset + block * block_rows) & (
            jnp.full(stack_shape, targets[slot], jnp.int32) >= 0
        )
        probs, score_grads = tile_weights(
            key_tile, value_tile, query_stack[...], grad_stack[...], total_row, delta_row, allowed, scale
        )
        vgrad_line[line, slot] = jnp.dot(probs, grad_stack[...], preferred_element_type=f32).astype(bf)
        kgrad_plane[place, slot] = (
            jnp.dot(score_grads, query_stack[...], preferred_element_type=f32) * scale
        ).astype(bf)
        late.append((score_grads, key_tile))
    spread(column, vgrad_line, vgrad_send_l, vgrad_recv_l)
    spread(plane, kgrad_plane, kgrad_send_p, kgrad_recv_p)
    for score_grads, key_tile in late:
        query_acc[...] += query_share(score_grads, key_tile, scale)
    stores = []
    for head in range(heads):
        store = pltpu.make_async_copy(
            query_acc.at[pl.ds(head * block_rows, block_rows), :],
            query_grad_hbm.at[:, pl.ds(head * head_width, head_width)],
            load_sem.at[len(loads) + head],
        )
        store.start()
        stores.append(store)

    def combine(group, info, held, held_count, first, step, out, target, send_sem, recv_sem):
        peer_of, count, _ = group
        for offset in list(range(1, count)) + [0]:
            peer, _ = peer_of(offset)
            sums = jnp.zeros(held.shape[2:], f32)
            for other in range(held_count):
                for slot in range(extra):
                    aimed = info[other, slot][0:1, :] == first + peer * step
                    sums = sums + jnp.where(aimed, held[other, slot].astype(f32), 0.0)
            if offset:
                out[peer] = sums.astype(bf)
                send(group, offset, out.at[peer], target, send_sem, recv_sem)
        return sums

    arrive(column, vgrad_line, vgrad_send_l, vgrad_recv_l)
    value_total = combine(plane, line_info, vgrad_line, line_count, line * plane_count, 1,
                          vgrad_plane_out, vgrad_plane, vgrad_send_p, vgrad_recv_p)
    arrive(plane, kgrad_plane, kgrad_send_p, kgrad_recv_p)
    key_total = combine(column, plane_info, kgrad_plane, plane_count, place, plane_count,
                        kgrad_line_out, kgrad_line, kgrad_send_l, kgrad_recv_l)
    value_total = value_total + value_acc[...]
    key_total = key_total + key_acc[...]
    arrive(column, kgrad_line, kgrad_send_l, kgrad_recv_l)
    for offset in range(1, line_count):
        key_total = key_total + kgrad_line[line_peer(offset)[0]].astype(f32)
    key_grad_ref[...] = key_total
    arrive(plane, vgrad_plane, vgrad_send_p, vgrad_recv_p)
    for offset in range(1, plane_count):
        value_total = value_total + vgrad_plane[plane_peer(offset)[0]].astype(f32)
    value_grad_ref[...] = value_total
    for copy in sent:
        copy.wait_send()
    for store in stores:
        store.wait()


def kernel_shards(query_rows, key_rows, value_rows, outputs, out_grads, log_totals, selected, counts):
    ka_count, pb_count = lax.axis_size("ka"), lax.axis_size("pb")
    inner = 2 if pb_count % 2 == 0 else 1
    line_count, plane_count = pb_count // inner, inner * ka_count
    extra = selected.shape[1] - 1
    block_rows, head_width = key_rows.shape
    heads = log_totals.shape[0]
    tile = key_rows.shape
    dma = pltpu.SemaphoreType.DMA
    vmem = pl.BlockSpec(memory_space=pltpu.VMEM)
    smem = pl.BlockSpec(memory_space=pltpu.SMEM)
    hbm = pl.BlockSpec(memory_space=pl.ANY)
    bf, f32 = jnp.bfloat16, jnp.float32
    return pl.pallas_call(
        functools.partial(whole_kernel, ka_count, inner, line_count, extra),
        out_shape=(
            jax.ShapeDtypeStruct(query_rows.shape, f32),
            jax.ShapeDtypeStruct(key_rows.shape, f32),
            jax.ShapeDtypeStruct(key_rows.shape, f32),
        ),
        in_specs=[hbm] * 6 + [smem] * 2,
        out_specs=(hbm, vmem, vmem),
        scratch_shapes=[
            pltpu.VMEM(query_rows.shape, bf),
            pltpu.VMEM(query_rows.shape, bf),
            pltpu.VMEM(query_rows.shape, bf),
            pltpu.VMEM(log_totals.shape, f32),
            pltpu.VMEM((plane_count, *tile), bf),
            pltpu.VMEM((line_count, extra, *tile), bf),
            pltpu.VMEM((line_count, extra, *tile), bf),
            pltpu.VMEM((line_count, *tile), bf),
            pltpu.VMEM((plane_count, extra, *tile), bf),
            pltpu.VMEM((plane_count, extra, *tile), bf),
            pltpu.VMEM((plane_count, extra, *tile), bf),
            pltpu.VMEM((line_count, *tile), bf),
            pltpu.VMEM((line_count, *tile), bf),
            pltpu.VMEM((line_count, extra, *tile), bf),
            pltpu.VMEM((plane_count, *tile), bf),
            pltpu.VMEM((plane_count, *tile), bf),
            pltpu.VMEM((plane_count, extra, 8, 128), jnp.int32),
            pltpu.VMEM((line_count, extra, 8, 128), jnp.int32),
            pltpu.VMEM((heads * block_rows, head_width), bf),
            pltpu.VMEM((heads * block_rows, head_width), bf),
            pltpu.VMEM((heads * block_rows, head_width), f32),
            pltpu.VMEM(tile, f32),
            pltpu.VMEM(tile, f32),
            *[dma((count,)) for count in (plane_count, plane_count, line_count, line_count) * 5],
            dma((6 + heads,)),
        ],
        compiler_params=pltpu.CompilerParams(collective_id=0, has_side_effects=True),
    )(query_rows, key_rows, value_rows, outputs, out_grads, log_totals, selected, counts)


def fits_kernel(query_rows, key_rows, value_rows, outputs, out_grads, log_totals, selected, counts):
    pb_count, ka_count = lax.axis_size("pb"), lax.axis_size("ka")
    block_rows, head_width = key_rows.shape
    inner = 2 if pb_count % 2 == 0 else 1
    extra = selected.shape[1] - 1
    tile_bytes = 2 * block_rows * head_width
    tiles = 3 * (pb_count // inner + inner * ka_count) * (1 + extra)
    return (
        selected.shape[0] == 1
        and extra > 0
        and block_rows == head_width == 128
        and tiles * tile_bytes < VMEM_BUDGET
    )


def either(*arrays):
    return kernel_shards(*arrays) if fits_kernel(*arrays) else shards(*arrays)


def solution(mesh):
    return jax.shard_map(
        either,
        mesh=mesh,
        in_specs=(
            P(("pb", "ka"), None),
            P(("pb", "ka"), None),
            P(("pb", "ka"), None),
            P(("pb", "ka"), None),
            P(("pb", "ka"), None),
            P(None, ("pb", "ka")),
            P(("pb", "ka"), None),
            P(("pb", "ka")),
        ),
        out_specs=(P(("pb", "ka"), None), P(("pb", "ka"), None), P(("pb", "ka"), None)),
        check_vma=False,
    )
```

```python
import functools

import jax
import jax.numpy as jnp
from jax import lax
from jax.experimental import pallas as pl
from jax.experimental.pallas import tpu as pltpu
from jax.sharding import PartitionSpec as P

VERY_LOW = -1e30


def passed_along(value, axis, steps):
    count = lax.axis_size(axis)
    pairs = [(source, (source + steps) % count) for source in range(count)]
    return lax.ppermute(value, axis, pairs)


def head_sums(grad_rows, out_rows, head_width):
    row_total = grad_rows.shape[0]
    part_heads = grad_rows.shape[1] // head_width
    product = grad_rows.astype(jnp.float32) * out_rows.astype(jnp.float32)
    return jnp.sum(product.reshape(row_total, part_heads, head_width), axis=2).T


def shards(query_rows, key_rows, value_rows, outputs, out_grads, log_totals, selected, counts):
    ka_count = lax.axis_size("ka")
    ka_index = lax.axis_index("ka")
    pb_index = lax.axis_index("pb")
    block_count = selected.shape[0]
    slot_count = selected.shape[1]
    head_width = key_rows.shape[1]
    block_rows = query_rows.shape[0] // block_count
    score_scale = head_width ** (-0.5)
    key_pairs = jnp.concatenate([key_rows, value_rows], 1)
    column_keys = lax.all_gather(key_pairs, "pb", axis=0, tiled=True)
    peer_slots, peer_counts = (
        lax.all_gather(selected, "ka", axis=0, tiled=True),
        lax.all_gather(counts, "ka", axis=0, tiled=True),
    )
    key_grads = jnp.zeros((column_keys.shape[0], 2 * head_width), jnp.float32)
    row_offsets = jnp.arange(block_rows, dtype=jnp.int32)
    flat_owner = jnp.repeat(jnp.arange(block_count, dtype=jnp.int32), slot_count)
    flat_slot = jnp.tile(jnp.arange(slot_count, dtype=jnp.int32), block_count)
    flat_places = jnp.arange(block_count * slot_count, dtype=jnp.int32)

    def visit_block(row_stack, query_grad, stat_stack, anchor, key_grads):
        held_query = row_stack[0]
        held_grad = row_stack[1]
        total_rows = stat_stack[0]
        delta_rows = head_sums(row_stack[1], row_stack[2], head_width)
        part_heads = total_rows.shape[0]
        held_slots = lax.dynamic_slice_in_dim(
            peer_slots, anchor * block_count, block_count, 0
        ).reshape(-1)
        held_counts = jnp.repeat(
            lax.dynamic_slice_in_dim(peer_counts, anchor * block_count, block_count, 0), slot_count
        )
        first_block = (pb_index * ka_count + anchor) * block_count
        wanted = (flat_slot < held_counts) & (held_slots // block_count % ka_count == ka_index)
        position = jnp.cumsum(wanted.astype(jnp.int32)) - 1
        placed = wanted[:, None] & (position[:, None] == flat_places[None, :])
        packed_ids = jnp.sum(jnp.where(placed, held_slots[:, None], 0), axis=0)
        packed_owner = jnp.sum(jnp.where(placed, flat_owner[:, None], 0), axis=0)
        live_tiles = jnp.sum(wanted.astype(jnp.int32))

        def one_tile(tile_index, loop_state):
            query_grad, key_grads = loop_state
            key_block = packed_ids[tile_index]
            owner_block = packed_owner[tile_index]
            key_start = (
                key_block // (block_count * ka_count) * block_count + key_block % block_count
            ) * block_rows
            pair_tile = lax.dynamic_slice_in_dim(column_keys, key_start, block_rows, 0)
            key_tile = pair_tile[:, :head_width]
            value_tile = pair_tile[:, head_width:]
            query_tile = held_query.reshape(block_rows, part_heads, head_width)
            grad_tile = held_grad.reshape(block_rows, part_heads, head_width)
            scores = (
                jnp.einsum("rhd,cd->hrc", query_tile, key_tile, preferred_element_type=jnp.float32)
                * score_scale
            )
            query_pos = (first_block + owner_block) * block_rows + row_offsets
            key_pos = key_block * block_rows + row_offsets
            allowed = key_pos[None, :] <= query_pos[:, None]
            probs_full = jnp.exp(
                jnp.where(allowed[None], scores - total_rows[:, :, None], VERY_LOW)
            )
            prob_grads = jnp.einsum(
                "rhd,cd->hrc", grad_tile, value_tile, preferred_element_type=jnp.float32
            )
            score_grads = probs_full * (prob_grads - delta_rows[:, :, None])
            rounded_probs = probs_full.astype(jnp.bfloat16)
            rounded_grads = score_grads.astype(jnp.bfloat16)
            value_part = jnp.einsum(
                "hrc,rhd->cd", rounded_probs, grad_tile, preferred_element_type=jnp.float32
            )
            key_part = (
                jnp.einsum(
                    "hrc,rhd->cd", rounded_grads, query_tile, preferred_element_type=jnp.float32
                )
                * score_scale
            )
            query_part = (
                jnp.einsum(
                    "hrc,cd->rhd", rounded_grads, key_tile, preferred_element_type=jnp.float32
                )
                * score_scale
            )
            old_query = query_grad
            query_grad = old_query + query_part.reshape(block_rows, -1)
            old_keys = lax.dynamic_slice_in_dim(key_grads, key_start, block_rows, 0)
            key_grads = lax.dynamic_update_slice_in_dim(
                key_grads, old_keys + jnp.concatenate([key_part, value_part], 1), key_start, 0
            )
            return (query_grad, key_grads)

        return lax.fori_loop(0, live_tiles, one_tile, (query_grad, key_grads))

    query_part = query_rows
    grad_zero = jnp.zeros(query_part.shape, jnp.float32)
    row_stack = jnp.stack([query_part, out_grads, outputs])
    query_grad = grad_zero
    stat_stack = log_totals[None]

    def forward_hop(hop_index, loop_state):
        row_stack, query_grad, stat_stack, key_grads = loop_state
        anchor = (ka_index - hop_index) % ka_count
        query_grad, key_grads = visit_block(row_stack, query_grad, stat_stack, anchor, key_grads)
        row_stack = passed_along(row_stack, "ka", 1)
        query_grad, stat_stack = passed_along((query_grad, stat_stack), "ka", 1)
        return (row_stack, query_grad, stat_stack, key_grads)

    row_stack, query_grad, stat_stack, key_grads = lax.fori_loop(
        0, ka_count - 1, forward_hop, (row_stack, query_grad, stat_stack, key_grads)
    )
    query_grad, key_grads = visit_block(
        row_stack, query_grad, stat_stack, (ka_index + 1) % ka_count, key_grads
    )
    query_grad = passed_along(query_grad, "ka", 1)
    owned_grads = lax.psum_scatter(key_grads, "pb", scatter_dimension=0, tiled=True)
    return (query_grad, owned_grads[:, :head_width], owned_grads[:, head_width:])


MESH = pl.DeviceIdType.MESH
VMEM_BUDGET = 40 << 20


def tile_weights(key_tile, value_tile, query_stack, grad_stack, total_row, delta_row, allowed, scale):
    nt = (((1,), (1,)), ((), ()))
    scores = lax.dot_general(key_tile, query_stack, nt, preferred_element_type=jnp.float32) * scale
    probs = jnp.exp(jnp.where(allowed, scores - total_row, VERY_LOW))
    prob_grads = lax.dot_general(value_tile, grad_stack, nt, preferred_element_type=jnp.float32)
    score_grads = probs * (prob_grads - delta_row)
    return probs.astype(jnp.bfloat16), score_grads.astype(jnp.bfloat16)


def query_share(score_grads, key_tile, scale):
    tn = (((0,), (0,)), ((), ()))
    return lax.dot_general(score_grads, key_tile, tn, preferred_element_type=jnp.float32) * scale


def whole_kernel(
    ka_count, inner, line_count, extra,
    query_hbm, key_hbm, value_hbm, out_hbm, grad_hbm, total_hbm, selected_ref, counts_ref,
    query_grad_ref, key_grad_ref, value_grad_ref,
    query_ref, out_ref, grad_ref, total_ref,
    key_plane, key_line, key_line_out, value_line, value_plane, value_plane_out,
    kgrad_plane, kgrad_line, kgrad_line_out, vgrad_line, vgrad_plane, vgrad_plane_out,
    plane_info, line_info, query_stack, grad_stack, query_acc, key_acc, value_acc,
    info_send_p, info_recv_p, info_send_l, info_recv_l,
    key_send_p, key_recv_p, key_send_l, key_recv_l,
    value_send_p, value_recv_p, value_send_l, value_recv_l,
    kgrad_send_p, kgrad_recv_p, kgrad_send_l, kgrad_recv_l,
    vgrad_send_p, vgrad_recv_p, vgrad_send_l, vgrad_recv_l,
    load_sem,
):
    bf, f32 = jnp.bfloat16, jnp.float32
    plane_count = inner * ka_count
    pb_index, ka_index = lax.axis_index("pb"), lax.axis_index("ka")
    line = lax.div(pb_index, inner)
    row = lax.rem(pb_index, inner)
    place = row * ka_count + ka_index
    block_rows, head_width = key_hbm.shape
    heads = total_hbm.shape[0]
    scale = head_width ** (-0.5)
    block = line * plane_count + place

    def plane_peer(offset):
        peer = lax.rem(place + offset, plane_count)
        return peer, (line * inner + lax.div(peer, ka_count), lax.rem(peer, ka_count))

    def line_peer(offset):
        peer = lax.rem(line + offset, line_count)
        return peer, (peer * inner + row, ka_index)

    plane = (plane_peer, plane_count, place)
    column = (line_peer, line_count, line)

    barrier = pltpu.get_barrier_semaphore()
    for peer_of, count, _ in (plane, column):
        for offset in range(1, count):
            pl.semaphore_signal(barrier, inc=1, device_id=peer_of(offset)[1], device_id_type=MESH)
    loads = [
        pltpu.make_async_copy(source, target, load_sem.at[index])
        for index, (source, target) in enumerate((
            (key_hbm, key_plane.at[place]), (value_hbm, value_line.at[line]),
            (query_hbm, query_ref), (grad_hbm, grad_ref), (out_hbm, out_ref), (total_hbm, total_ref),
        ))
    ]
    for load in loads:
        load.start()

    targets = [
        jnp.where(slot + 1 < counts_ref[0], selected_ref[0, slot + 1], -1) for slot in range(extra)
    ]
    for slot in range(extra):
        lines = jnp.full((8, 128), targets[slot], jnp.int32)
        plane_info[place, slot] = lines
        line_info[line, slot] = lines

    sent = []

    def send(group, offset, source, target, send_sem, recv_sem):
        peer_of, _, me = group
        copy = pltpu.make_async_remote_copy(
            src_ref=source, dst_ref=target.at[me], send_sem=send_sem.at[offset],
            recv_sem=recv_sem.at[me], device_id=peer_of(offset)[1], device_id_type=MESH,
        )
        copy.start()
        sent.append(copy)

    def spread(group, target, send_sem, recv_sem):
        for offset in range(1, group[1]):
            send(group, offset, target.at[group[2]], target, send_sem, recv_sem)

    def arrive(group, target, send_sem, recv_sem):
        peer_of, count, _ = group
        for offset in range(1, count):
            peer, device = peer_of(offset)
            pltpu.make_async_remote_copy(
                src_ref=target.at[peer], dst_ref=target.at[peer], send_sem=send_sem.at[offset],
                recv_sem=recv_sem.at[peer], device_id=device, device_id_type=MESH,
            ).wait_recv()

    loads[0].wait()
    loads[1].wait()
    pl.semaphore_wait(barrier, plane_count + line_count - 2)
    spread(column, line_info, info_send_l, info_recv_l)
    spread(plane, plane_info, info_send_p, info_recv_p)
    spread(column, value_line, value_send_l, value_recv_l)
    spread(plane, key_plane, key_send_p, key_recv_p)

    for load in loads[2:]:
        load.wait()
    deltas = []
    for head in range(heads):
        columns = pl.ds(head * head_width, head_width)
        rows = pl.ds(head * block_rows, block_rows)
        query_stack[rows, :] = query_ref[:, columns]
        grad_stack[rows, :] = grad_ref[:, columns]
        product = grad_ref[:, columns].astype(f32) * out_ref[:, columns].astype(f32)
        deltas.append(jnp.sum(product.T, axis=0, keepdims=True))
    delta_row = jnp.concatenate(deltas, axis=1)
    total_row = jnp.concatenate([total_ref[head : head + 1, :] for head in range(heads)], axis=1)
    stack_shape = (block_rows, heads * block_rows)
    key_offset = lax.broadcasted_iota(jnp.int32, stack_shape, 0)
    query_offset = lax.rem(lax.broadcasted_iota(jnp.int32, stack_shape, 1), block_rows)

    arrive(column, line_info, info_send_l, info_recv_l)
    arrive(plane, plane_info, info_send_p, info_recv_p)

    def pick(group, info, held, held_count, first, step, out, target, send_sem, recv_sem):
        peer_of, count, me = group
        for offset in list(range(1, count)) + [0]:
            peer, _ = peer_of(offset)
            for slot in range(extra):
                wanted = info[peer, slot][0:1, :]
                picked = jnp.zeros(held.shape[1:], f32)
                for other in range(held_count):
                    picked = jnp.where(wanted == first + other * step, held[other].astype(f32), picked)
                if offset:
                    out[peer, slot] = picked.astype(bf)
                else:
                    target[me, slot] = picked.astype(bf)
            if offset:
                send(group, offset, out.at[peer], target, send_sem, recv_sem)

    arrive(column, value_line, value_send_l, value_recv_l)
    pick(plane, plane_info, value_line, line_count, place, plane_count,
         value_plane_out, value_plane, value_send_p, value_recv_p)
    arrive(plane, key_plane, key_send_p, key_recv_p)
    pick(column, line_info, key_plane, plane_count, line * plane_count, 1,
         key_line_out, key_line, key_send_l, key_recv_l)

    own_key = key_plane[place]
    probs, score_grads = tile_weights(
        own_key, value_line[line], query_stack[...], grad_stack[...], total_row, delta_row,
        key_offset <= query_offset, scale,
    )
    query_acc[...] = query_share(score_grads, own_key, scale)
    key_acc[...] = jnp.dot(score_grads, query_stack[...], preferred_element_type=f32) * scale
    value_acc[...] = jnp.dot(probs, grad_stack[...], preferred_element_type=f32)

    arrive(column, key_line, key_send_l, key_recv_l)
    arrive(plane, value_plane, value_send_p, value_recv_p)
    late = []
    for slot in range(extra):
        listed = jnp.maximum(targets[slot], 0)
        key_tile = key_line[lax.div(listed, plane_count), slot]
        value_tile = value_plane[lax.rem(listed, plane_count), slot]
        allowed = (key_offset + targets[slot] * block_rows <= query_offset + block * block_rows) & (
            jnp.full(stack_shape, targets[slot], jnp.int32) >= 0
        )
        probs, score_grads = tile_weights(
            key_tile, value_tile, query_stack[...], grad_stack[...], total_row, delta_row, allowed, scale
        )
        vgrad_line[line, slot] = jnp.dot(probs, grad_stack[...], preferred_element_type=f32).astype(bf)
        kgrad_plane[place, slot] = (
            jnp.dot(score_grads, query_stack[...], preferred_element_type=f32) * scale
        ).astype(bf)
        late.append((score_grads, key_tile))
    spread(column, vgrad_line, vgrad_send_l, vgrad_recv_l)
    spread(plane, kgrad_plane, kgrad_send_p, kgrad_recv_p)
    for score_grads, key_tile in late:
        query_acc[...] += query_share(score_grads, key_tile, scale)
    for head in range(heads):
        query_grad_ref[:, pl.ds(head * head_width, head_width)] = query_acc[
            pl.ds(head * block_rows, block_rows), :
        ]

    def combine(group, info, held, held_count, first, step, out, target, send_sem, recv_sem):
        peer_of, count, _ = group
        for offset in list(range(1, count)) + [0]:
            peer, _ = peer_of(offset)
            sums = jnp.zeros(held.shape[2:], f32)
            for other in range(held_count):
                for slot in range(extra):
                    aimed = info[other, slot][0:1, :] == first + peer * step
                    sums = sums + jnp.where(aimed, held[other, slot].astype(f32), 0.0)
            if offset:
                out[peer] = sums.astype(bf)
                send(group, offset, out.at[peer], target, send_sem, recv_sem)
        return sums

    arrive(column, vgrad_line, vgrad_send_l, vgrad_recv_l)
    value_total = combine(plane, line_info, vgrad_line, line_count, line * plane_count, 1,
                          vgrad_plane_out, vgrad_plane, vgrad_send_p, vgrad_recv_p)
    arrive(plane, kgrad_plane, kgrad_send_p, kgrad_recv_p)
    key_total = combine(column, plane_info, kgrad_plane, plane_count, place, plane_count,
                        kgrad_line_out, kgrad_line, kgrad_send_l, kgrad_recv_l)
    value_total = value_total + value_acc[...]
    key_total = key_total + key_acc[...]
    arrive(column, kgrad_line, kgrad_send_l, kgrad_recv_l)
    for offset in range(1, line_count):
        key_total = key_total + kgrad_line[line_peer(offset)[0]].astype(f32)
    key_grad_ref[...] = key_total
    arrive(plane, vgrad_plane, vgrad_send_p, vgrad_recv_p)
    for offset in range(1, plane_count):
        value_total = value_total + vgrad_plane[plane_peer(offset)[0]].astype(f32)
    value_grad_ref[...] = value_total
    for copy in sent:
        copy.wait_send()


def kernel_shards(query_rows, key_rows, value_rows, outputs, out_grads, log_totals, selected, counts):
    ka_count, pb_count = lax.axis_size("ka"), lax.axis_size("pb")
    inner = 2 if pb_count % 2 == 0 else 1
    line_count, plane_count = pb_count // inner, inner * ka_count
    extra = selected.shape[1] - 1
    block_rows, head_width = key_rows.shape
    heads = log_totals.shape[0]
    tile = key_rows.shape
    dma = pltpu.SemaphoreType.DMA
    vmem = pl.BlockSpec(memory_space=pltpu.VMEM)
    smem = pl.BlockSpec(memory_space=pltpu.SMEM)
    hbm = pl.BlockSpec(memory_space=pl.ANY)
    bf, f32 = jnp.bfloat16, jnp.float32
    shapes = (query_rows.shape, key_rows.shape, value_rows.shape)
    held = pl.pallas_call(
        functools.partial(whole_kernel, ka_count, inner, line_count, extra),
        out_shape=tuple(pltpu.VMEM(shape, f32) for shape in shapes),
        in_specs=[hbm] * 6 + [smem] * 2,
        out_specs=(vmem, vmem, vmem),
        scratch_shapes=[
            pltpu.VMEM(query_rows.shape, bf),
            pltpu.VMEM(query_rows.shape, bf),
            pltpu.VMEM(query_rows.shape, bf),
            pltpu.VMEM(log_totals.shape, f32),
            pltpu.VMEM((plane_count, *tile), bf),
            pltpu.VMEM((line_count, extra, *tile), bf),
            pltpu.VMEM((line_count, extra, *tile), bf),
            pltpu.VMEM((line_count, *tile), bf),
            pltpu.VMEM((plane_count, extra, *tile), bf),
            pltpu.VMEM((plane_count, extra, *tile), bf),
            pltpu.VMEM((plane_count, extra, *tile), bf),
            pltpu.VMEM((line_count, *tile), bf),
            pltpu.VMEM((line_count, *tile), bf),
            pltpu.VMEM((line_count, extra, *tile), bf),
            pltpu.VMEM((plane_count, *tile), bf),
            pltpu.VMEM((plane_count, *tile), bf),
            pltpu.VMEM((plane_count, extra, 8, 128), jnp.int32),
            pltpu.VMEM((line_count, extra, 8, 128), jnp.int32),
            pltpu.VMEM((heads * block_rows, head_width), bf),
            pltpu.VMEM((heads * block_rows, head_width), bf),
            pltpu.VMEM((heads * block_rows, head_width), f32),
            pltpu.VMEM(tile, f32),
            pltpu.VMEM(tile, f32),
            *[dma((count,)) for count in (plane_count, plane_count, line_count, line_count) * 5],
            dma((6,)),
        ],
        compiler_params=pltpu.CompilerParams(collective_id=0, has_side_effects=True),
    )(query_rows, key_rows, value_rows, outputs, out_grads, log_totals, selected, counts)
    return pl.pallas_call(
        write_kernel,
        out_shape=tuple(jax.ShapeDtypeStruct(shape, f32) for shape in shapes),
        in_specs=[vmem] * 3,
        out_specs=(hbm, hbm, hbm),
        scratch_shapes=[dma((3,))],
    )(*[pltpu.with_memory_space_constraint(part, pltpu.VMEM) for part in held])


def write_kernel(*refs):
    sources, targets, sem = refs[:3], refs[3:6], refs[6]
    stores = [pltpu.make_async_copy(*pair, sem.at[i]) for i, pair in enumerate(zip(sources, targets))]
    for store in stores:
        store.start()
    for store in stores:
        store.wait()


def fits_kernel(query_rows, key_rows, value_rows, outputs, out_grads, log_totals, selected, counts):
    pb_count, ka_count = lax.axis_size("pb"), lax.axis_size("ka")
    block_rows, head_width = key_rows.shape
    inner = 2 if pb_count % 2 == 0 else 1
    extra = selected.shape[1] - 1
    tile_bytes = 2 * block_rows * head_width
    tiles = 3 * (pb_count // inner + inner * ka_count) * (1 + extra)
    return (
        selected.shape[0] == 1
        and extra > 0
        and block_rows == head_width == 128
        and tiles * tile_bytes < VMEM_BUDGET
    )


def either(*arrays):
    return kernel_shards(*arrays) if fits_kernel(*arrays) else shards(*arrays)


def solution(mesh):
    return jax.shard_map(
        either,
        mesh=mesh,
        in_specs=(
            P(("pb", "ka"), None),
            P(("pb", "ka"), None),
            P(("pb", "ka"), None),
            P(("pb", "ka"), None),
            P(("pb", "ka"), None),
            P(None, ("pb", "ka")),
            P(("pb", "ka"), None),
            P(("pb", "ka")),
        ),
        out_specs=(P(("pb", "ka"), None), P(("pb", "ka"), None), P(("pb", "ka"), None)),
        check_vma=False,
    )
```

```python
import functools

import jax
import jax.numpy as jnp
from jax import lax
from jax.experimental import pallas as pl
from jax.experimental.pallas import tpu as pltpu
from jax.sharding import PartitionSpec as P

VERY_LOW = -1e30


def passed_along(value, axis, steps):
    count = lax.axis_size(axis)
    pairs = [(source, (source + steps) % count) for source in range(count)]
    return lax.ppermute(value, axis, pairs)


def head_sums(grad_rows, out_rows, head_width):
    row_total = grad_rows.shape[0]
    part_heads = grad_rows.shape[1] // head_width
    product = grad_rows.astype(jnp.float32) * out_rows.astype(jnp.float32)
    return jnp.sum(product.reshape(row_total, part_heads, head_width), axis=2).T


def shards(query_rows, key_rows, value_rows, outputs, out_grads, log_totals, selected, counts):
    ka_count = lax.axis_size("ka")
    ka_index = lax.axis_index("ka")
    pb_index = lax.axis_index("pb")
    block_count = selected.shape[0]
    slot_count = selected.shape[1]
    head_width = key_rows.shape[1]
    block_rows = query_rows.shape[0] // block_count
    score_scale = head_width ** (-0.5)
    key_pairs = jnp.concatenate([key_rows, value_rows], 1)
    column_keys = lax.all_gather(key_pairs, "pb", axis=0, tiled=True)
    peer_slots, peer_counts = (
        lax.all_gather(selected, "ka", axis=0, tiled=True),
        lax.all_gather(counts, "ka", axis=0, tiled=True),
    )
    key_grads = jnp.zeros((column_keys.shape[0], 2 * head_width), jnp.float32)
    row_offsets = jnp.arange(block_rows, dtype=jnp.int32)
    flat_owner = jnp.repeat(jnp.arange(block_count, dtype=jnp.int32), slot_count)
    flat_slot = jnp.tile(jnp.arange(slot_count, dtype=jnp.int32), block_count)
    flat_places = jnp.arange(block_count * slot_count, dtype=jnp.int32)

    def visit_block(row_stack, query_grad, stat_stack, anchor, key_grads):
        held_query = row_stack[0]
        held_grad = row_stack[1]
        total_rows = stat_stack[0]
        delta_rows = head_sums(row_stack[1], row_stack[2], head_width)
        part_heads = total_rows.shape[0]
        held_slots = lax.dynamic_slice_in_dim(
            peer_slots, anchor * block_count, block_count, 0
        ).reshape(-1)
        held_counts = jnp.repeat(
            lax.dynamic_slice_in_dim(peer_counts, anchor * block_count, block_count, 0), slot_count
        )
        first_block = (pb_index * ka_count + anchor) * block_count
        wanted = (flat_slot < held_counts) & (held_slots // block_count % ka_count == ka_index)
        position = jnp.cumsum(wanted.astype(jnp.int32)) - 1
        placed = wanted[:, None] & (position[:, None] == flat_places[None, :])
        packed_ids = jnp.sum(jnp.where(placed, held_slots[:, None], 0), axis=0)
        packed_owner = jnp.sum(jnp.where(placed, flat_owner[:, None], 0), axis=0)
        live_tiles = jnp.sum(wanted.astype(jnp.int32))

        def one_tile(tile_index, loop_state):
            query_grad, key_grads = loop_state
            key_block = packed_ids[tile_index]
            owner_block = packed_owner[tile_index]
            key_start = (
                key_block // (block_count * ka_count) * block_count + key_block % block_count
            ) * block_rows
            pair_tile = lax.dynamic_slice_in_dim(column_keys, key_start, block_rows, 0)
            key_tile = pair_tile[:, :head_width]
            value_tile = pair_tile[:, head_width:]
            query_tile = held_query.reshape(block_rows, part_heads, head_width)
            grad_tile = held_grad.reshape(block_rows, part_heads, head_width)
            scores = (
                jnp.einsum("rhd,cd->hrc", query_tile, key_tile, preferred_element_type=jnp.float32)
                * score_scale
            )
            query_pos = (first_block + owner_block) * block_rows + row_offsets
            key_pos = key_block * block_rows + row_offsets
            allowed = key_pos[None, :] <= query_pos[:, None]
            probs_full = jnp.exp(
                jnp.where(allowed[None], scores - total_rows[:, :, None], VERY_LOW)
            )
            prob_grads = jnp.einsum(
                "rhd,cd->hrc", grad_tile, value_tile, preferred_element_type=jnp.float32
            )
            score_grads = probs_full * (prob_grads - delta_rows[:, :, None])
            rounded_probs = probs_full.astype(jnp.bfloat16)
            rounded_grads = score_grads.astype(jnp.bfloat16)
            value_part = jnp.einsum(
                "hrc,rhd->cd", rounded_probs, grad_tile, preferred_element_type=jnp.float32
            )
            key_part = (
                jnp.einsum(
                    "hrc,rhd->cd", rounded_grads, query_tile, preferred_element_type=jnp.float32
                )
                * score_scale
            )
            query_part = (
                jnp.einsum(
                    "hrc,cd->rhd", rounded_grads, key_tile, preferred_element_type=jnp.float32
                )
                * score_scale
            )
            old_query = query_grad
            query_grad = old_query + query_part.reshape(block_rows, -1)
            old_keys = lax.dynamic_slice_in_dim(key_grads, key_start, block_rows, 0)
            key_grads = lax.dynamic_update_slice_in_dim(
                key_grads, old_keys + jnp.concatenate([key_part, value_part], 1), key_start, 0
            )
            return (query_grad, key_grads)

        return lax.fori_loop(0, live_tiles, one_tile, (query_grad, key_grads))

    query_part = query_rows
    grad_zero = jnp.zeros(query_part.shape, jnp.float32)
    row_stack = jnp.stack([query_part, out_grads, outputs])
    query_grad = grad_zero
    stat_stack = log_totals[None]

    def forward_hop(hop_index, loop_state):
        row_stack, query_grad, stat_stack, key_grads = loop_state
        anchor = (ka_index - hop_index) % ka_count
        query_grad, key_grads = visit_block(row_stack, query_grad, stat_stack, anchor, key_grads)
        row_stack = passed_along(row_stack, "ka", 1)
        query_grad, stat_stack = passed_along((query_grad, stat_stack), "ka", 1)
        return (row_stack, query_grad, stat_stack, key_grads)

    row_stack, query_grad, stat_stack, key_grads = lax.fori_loop(
        0, ka_count - 1, forward_hop, (row_stack, query_grad, stat_stack, key_grads)
    )
    query_grad, key_grads = visit_block(
        row_stack, query_grad, stat_stack, (ka_index + 1) % ka_count, key_grads
    )
    query_grad = passed_along(query_grad, "ka", 1)
    owned_grads = lax.psum_scatter(key_grads, "pb", scatter_dimension=0, tiled=True)
    return (query_grad, owned_grads[:, :head_width], owned_grads[:, head_width:])


MESH = pl.DeviceIdType.MESH
VMEM_BUDGET = 40 << 20


def tile_weights(key_tile, value_tile, query_stack, grad_stack, total_row, delta_row, allowed, scale):
    nt = (((1,), (1,)), ((), ()))
    scores = lax.dot_general(key_tile, query_stack, nt, preferred_element_type=jnp.float32) * scale
    probs = jnp.exp(jnp.where(allowed, scores - total_row, VERY_LOW))
    prob_grads = lax.dot_general(value_tile, grad_stack, nt, preferred_element_type=jnp.float32)
    score_grads = probs * (prob_grads - delta_row)
    return probs.astype(jnp.bfloat16), score_grads.astype(jnp.bfloat16)


def query_share(score_grads, key_tile, scale):
    tn = (((0,), (0,)), ((), ()))
    return lax.dot_general(score_grads, key_tile, tn, preferred_element_type=jnp.float32) * scale


def whole_kernel(
    ka_count, inner, line_count, extra, chunks,
    query_hbm, key_hbm, value_hbm, out_hbm, grad_hbm, total_hbm, selected_ref, counts_ref,
    query_grad_ref, key_grad_ref, value_grad_ref,
    query_ref, out_ref, grad_ref, total_ref,
    key_plane, key_line, key_line_out, value_line, value_plane, value_plane_out,
    kgrad_plane, kgrad_line, kgrad_line_out, vgrad_line, vgrad_plane, vgrad_plane_out,
    plane_info, line_info, query_stack, grad_stack, query_acc, key_acc, value_acc,
    info_send_p, info_recv_p, info_send_l, info_recv_l,
    key_send_p, key_recv_p, key_send_l, key_recv_l,
    value_send_p, value_recv_p, value_send_l, value_recv_l,
    kgrad_send_p, kgrad_recv_p, kgrad_send_l, kgrad_recv_l,
    vgrad_send_p, vgrad_recv_p, vgrad_send_l, vgrad_recv_l,
    load_sem,
):
    bf, f32 = jnp.bfloat16, jnp.float32
    plane_count = inner * ka_count
    pb_index, ka_index = lax.axis_index("pb"), lax.axis_index("ka")
    line = lax.div(pb_index, inner)
    row = lax.rem(pb_index, inner)
    place = row * ka_count + ka_index
    block_rows, head_width = key_hbm.shape
    heads = total_hbm.shape[0]
    scale = head_width ** (-0.5)
    chunk_rows = block_rows // chunks
    spans = [pl.ds(chunk * chunk_rows, chunk_rows) for chunk in range(chunks)]
    block = line * plane_count + place

    def plane_peer(offset):
        peer = lax.rem(place + offset, plane_count)
        return peer, (line * inner + lax.div(peer, ka_count), lax.rem(peer, ka_count))

    def line_peer(offset):
        peer = lax.rem(line + offset, line_count)
        return peer, (peer * inner + row, ka_index)

    plane = (plane_peer, plane_count, place)
    column = (line_peer, line_count, line)

    barrier = pltpu.get_barrier_semaphore()
    for peer_of, count, _ in (plane, column):
        for offset in range(1, count):
            pl.semaphore_signal(barrier, inc=1, device_id=peer_of(offset)[1], device_id_type=MESH)
    moves = []
    for chunk, span in enumerate(spans):
        moves.append((key_hbm.at[span], key_plane.at[place, chunk]))
        moves.append((value_hbm.at[span], value_line.at[line, chunk]))
    moves += [(query_hbm, query_ref), (grad_hbm, grad_ref), (out_hbm, out_ref), (total_hbm, total_ref)]
    loads = [
        pltpu.make_async_copy(*move, load_sem.at[index]) for index, move in enumerate(moves)
    ]
    for load in loads:
        load.start()

    targets = [
        jnp.where(slot + 1 < counts_ref[0], selected_ref[0, slot + 1], -1) for slot in range(extra)
    ]
    for slot in range(extra):
        lines = jnp.full((8, 128), targets[slot], jnp.int32)
        plane_info[place, 0, slot] = lines
        line_info[line, 0, slot] = lines

    sent = []

    def send(group, offset, chunk, source, target, send_sem, recv_sem):
        peer_of, _, me = group
        copy = pltpu.make_async_remote_copy(
            src_ref=source, dst_ref=target.at[me, chunk], send_sem=send_sem.at[offset, chunk],
            recv_sem=recv_sem.at[me, chunk], device_id=peer_of(offset)[1], device_id_type=MESH,
        )
        copy.start()
        sent.append(copy)

    def spread(group, chunk, target, send_sem, recv_sem):
        for offset in range(1, group[1]):
            send(group, offset, chunk, target.at[group[2], chunk], target, send_sem, recv_sem)

    def arrive(group, chunk, target, send_sem, recv_sem):
        peer_of, count, _ = group
        for offset in range(1, count):
            peer, device = peer_of(offset)
            pltpu.make_async_remote_copy(
                src_ref=target.at[peer, chunk], dst_ref=target.at[peer, chunk],
                send_sem=send_sem.at[offset, chunk], recv_sem=recv_sem.at[peer, chunk],
                device_id=device, device_id_type=MESH,
            ).wait_recv()

    for load in loads[: 2 * chunks]:
        load.wait()
    pl.semaphore_wait(barrier, plane_count + line_count - 2)
    spread(column, 0, line_info, info_send_l, info_recv_l)
    spread(plane, 0, plane_info, info_send_p, info_recv_p)
    for chunk in range(chunks):
        spread(column, chunk, value_line, value_send_l, value_recv_l)
        spread(plane, chunk, key_plane, key_send_p, key_recv_p)

    for load in loads[2 * chunks :]:
        load.wait()
    deltas = []
    for head in range(heads):
        columns = pl.ds(head * head_width, head_width)
        rows = pl.ds(head * block_rows, block_rows)
        query_stack[rows, :] = query_ref[:, columns]
        grad_stack[rows, :] = grad_ref[:, columns]
        product = grad_ref[:, columns].astype(f32) * out_ref[:, columns].astype(f32)
        deltas.append(jnp.sum(product.T, axis=0, keepdims=True))
    delta_row = jnp.concatenate(deltas, axis=1)
    total_row = jnp.concatenate([total_ref[head : head + 1, :] for head in range(heads)], axis=1)
    stack_shape = (block_rows, heads * block_rows)
    key_offset = lax.broadcasted_iota(jnp.int32, stack_shape, 0)
    query_offset = lax.rem(lax.broadcasted_iota(jnp.int32, stack_shape, 1), block_rows)

    arrive(column, 0, line_info, info_send_l, info_recv_l)
    arrive(plane, 0, plane_info, info_send_p, info_recv_p)

    def pick(group, chunk, info, held, held_count, first, step, out, target, send_sem, recv_sem):
        peer_of, count, me = group
        for offset in list(range(1, count)) + [0]:
            peer, _ = peer_of(offset)
            for slot in range(extra):
                wanted = info[peer, 0, slot][0:1, :]
                picked = jnp.zeros(held.shape[2:], f32)
                for other in range(held_count):
                    picked = jnp.where(
                        wanted == first + other * step, held[other, chunk].astype(f32), picked
                    )
                if offset:
                    out[peer, chunk, slot] = picked.astype(bf)
                else:
                    target[me, chunk, slot] = picked.astype(bf)
            if offset:
                send(group, offset, chunk, out.at[peer, chunk], target, send_sem, recv_sem)

    for chunk in range(chunks):
        arrive(column, chunk, value_line, value_send_l, value_recv_l)
        pick(plane, chunk, plane_info, value_line, line_count, place, plane_count,
             value_plane_out, value_plane, value_send_p, value_recv_p)
        arrive(plane, chunk, key_plane, key_send_p, key_recv_p)
        pick(column, chunk, line_info, key_plane, plane_count, line * plane_count, 1,
             key_line_out, key_line, key_send_l, key_recv_l)

    def whole(parts):
        return jnp.concatenate(parts, axis=0)

    own_key = whole([key_plane[place, chunk] for chunk in range(chunks)])
    own_value = whole([value_line[line, chunk] for chunk in range(chunks)])
    probs, score_grads = tile_weights(
        own_key, own_value, query_stack[...], grad_stack[...], total_row, delta_row,
        key_offset <= query_offset, scale,
    )
    query_acc[...] = query_share(score_grads, own_key, scale)
    key_acc[...] = jnp.dot(score_grads, query_stack[...], preferred_element_type=f32) * scale
    value_acc[...] = jnp.dot(probs, grad_stack[...], preferred_element_type=f32)

    for chunk in range(chunks):
        arrive(column, chunk, key_line, key_send_l, key_recv_l)
        arrive(plane, chunk, value_plane, value_send_p, value_recv_p)
    late = []
    for slot in range(extra):
        listed = jnp.maximum(targets[slot], 0)
        source, spot = lax.div(listed, plane_count), lax.rem(listed, plane_count)
        key_tile = whole([key_line[source, chunk, slot] for chunk in range(chunks)])
        value_tile = whole([value_plane[spot, chunk, slot] for chunk in range(chunks)])
        allowed = (key_offset + targets[slot] * block_rows <= query_offset + block * block_rows) & (
            jnp.full(stack_shape, targets[slot], jnp.int32) >= 0
        )
        probs, score_grads = tile_weights(
            key_tile, value_tile, query_stack[...], grad_stack[...], total_row, delta_row, allowed, scale
        )
        value_part = jnp.dot(probs, grad_stack[...], preferred_element_type=f32).astype(bf)
        key_part = (jnp.dot(score_grads, query_stack[...], preferred_element_type=f32) * scale).astype(bf)
        for chunk in range(chunks):
            rows = slice(chunk * chunk_rows, (chunk + 1) * chunk_rows)
            vgrad_line[line, chunk, slot] = value_part[rows]
            kgrad_plane[place, chunk, slot] = key_part[rows]
        late.append((score_grads, key_tile))
    for chunk in range(chunks):
        spread(column, chunk, vgrad_line, vgrad_send_l, vgrad_recv_l)
        spread(plane, chunk, kgrad_plane, kgrad_send_p, kgrad_recv_p)
    for score_grads, key_tile in late:
        query_acc[...] += query_share(score_grads, key_tile, scale)
    for head in range(heads):
        query_grad_ref[:, pl.ds(head * head_width, head_width)] = query_acc[
            pl.ds(head * block_rows, block_rows), :
        ]

    def combine(group, chunk, info, held, held_count, first, step, out, target, send_sem, recv_sem):
        peer_of, count, _ = group
        for offset in list(range(1, count)) + [0]:
            peer, _ = peer_of(offset)
            sums = jnp.zeros(held.shape[3:], f32)
            for other in range(held_count):
                for slot in range(extra):
                    aimed = info[other, 0, slot][0:1, :] == first + peer * step
                    sums = sums + jnp.where(aimed, held[other, chunk, slot].astype(f32), 0.0)
            if offset:
                out[peer, chunk] = sums.astype(bf)
                send(group, offset, chunk, out.at[peer, chunk], target, send_sem, recv_sem)
        return sums

    for chunk, span in enumerate(spans):
        arrive(column, chunk, vgrad_line, vgrad_send_l, vgrad_recv_l)
        value_acc[span, :] += combine(
            plane, chunk, line_info, vgrad_line, line_count, line * plane_count, 1,
            vgrad_plane_out, vgrad_plane, vgrad_send_p, vgrad_recv_p)
        arrive(plane, chunk, kgrad_plane, kgrad_send_p, kgrad_recv_p)
        key_acc[span, :] += combine(
            column, chunk, plane_info, kgrad_plane, plane_count, place, plane_count,
            kgrad_line_out, kgrad_line, kgrad_send_l, kgrad_recv_l)

    def finish(group, chunk, span, total, target, send_sem, recv_sem, result_ref):
        arrive(group, chunk, target, send_sem, recv_sem)
        sums = total[span, :]
        for offset in range(1, group[1]):
            sums = sums + target[group[0](offset)[0], chunk].astype(f32)
        result_ref[span, :] = sums

    for chunk, span in enumerate(spans):
        finish(plane, chunk, span, value_acc, vgrad_plane, vgrad_send_p, vgrad_recv_p, value_grad_ref)
        finish(column, chunk, span, key_acc, kgrad_line, kgrad_send_l, kgrad_recv_l, key_grad_ref)
    for copy in sent:
        copy.wait_send()


def kernel_shards(query_rows, key_rows, value_rows, outputs, out_grads, log_totals, selected, counts):
    ka_count, pb_count = lax.axis_size("ka"), lax.axis_size("pb")
    inner = 2 if pb_count % 2 == 0 else 1
    line_count, plane_count = pb_count // inner, inner * ka_count
    extra = selected.shape[1] - 1
    block_rows, head_width = key_rows.shape
    heads = log_totals.shape[0]
    chunks = 2
    tile = (block_rows // chunks, head_width)
    dma = pltpu.SemaphoreType.DMA
    vmem = pl.BlockSpec(memory_space=pltpu.VMEM)
    smem = pl.BlockSpec(memory_space=pltpu.SMEM)
    hbm = pl.BlockSpec(memory_space=pl.ANY)
    bf, f32 = jnp.bfloat16, jnp.float32
    shapes = (query_rows.shape, key_rows.shape, value_rows.shape)
    held = pl.pallas_call(
        functools.partial(whole_kernel, ka_count, inner, line_count, extra, chunks),
        out_shape=tuple(pltpu.VMEM(shape, f32) for shape in shapes),
        in_specs=[hbm] * 6 + [smem] * 2,
        out_specs=(vmem, vmem, vmem),
        scratch_shapes=[
            pltpu.VMEM(query_rows.shape, bf),
            pltpu.VMEM(query_rows.shape, bf),
            pltpu.VMEM(query_rows.shape, bf),
            pltpu.VMEM(log_totals.shape, f32),
            pltpu.VMEM((plane_count, chunks, *tile), bf),
            pltpu.VMEM((line_count, chunks, extra, *tile), bf),
            pltpu.VMEM((line_count, chunks, extra, *tile), bf),
            pltpu.VMEM((line_count, chunks, *tile), bf),
            pltpu.VMEM((plane_count, chunks, extra, *tile), bf),
            pltpu.VMEM((plane_count, chunks, extra, *tile), bf),
            pltpu.VMEM((plane_count, chunks, extra, *tile), bf),
            pltpu.VMEM((line_count, chunks, *tile), bf),
            pltpu.VMEM((line_count, chunks, *tile), bf),
            pltpu.VMEM((line_count, chunks, extra, *tile), bf),
            pltpu.VMEM((plane_count, chunks, *tile), bf),
            pltpu.VMEM((plane_count, chunks, *tile), bf),
            pltpu.VMEM((plane_count, 1, extra, 8, 128), jnp.int32),
            pltpu.VMEM((line_count, 1, extra, 8, 128), jnp.int32),
            pltpu.VMEM((heads * block_rows, head_width), bf),
            pltpu.VMEM((heads * block_rows, head_width), bf),
            pltpu.VMEM((heads * block_rows, head_width), f32),
            pltpu.VMEM(key_rows.shape, f32),
            pltpu.VMEM(key_rows.shape, f32),
            *[dma((count, chunks)) for count in (plane_count, plane_count, line_count, line_count) * 5],
            dma((2 * chunks + 4,)),
        ],
        compiler_params=pltpu.CompilerParams(collective_id=0, has_side_effects=True),
    )(query_rows, key_rows, value_rows, outputs, out_grads, log_totals, selected, counts)
    return pl.pallas_call(
        write_kernel,
        out_shape=tuple(jax.ShapeDtypeStruct(shape, f32) for shape in shapes),
        in_specs=[vmem] * 3,
        out_specs=(hbm, hbm, hbm),
        scratch_shapes=[dma((3,))],
    )(*[pltpu.with_memory_space_constraint(part, pltpu.VMEM) for part in held])


def write_kernel(*refs):
    sources, targets, sem = refs[:3], refs[3:6], refs[6]
    stores = [pltpu.make_async_copy(*pair, sem.at[i]) for i, pair in enumerate(zip(sources, targets))]
    for store in stores:
        store.start()
    for store in stores:
        store.wait()


def fits_kernel(query_rows, key_rows, value_rows, outputs, out_grads, log_totals, selected, counts):
    pb_count, ka_count = lax.axis_size("pb"), lax.axis_size("ka")
    block_rows, head_width = key_rows.shape
    inner = 2 if pb_count % 2 == 0 else 1
    extra = selected.shape[1] - 1
    tile_bytes = 2 * block_rows * head_width
    tiles = 3 * (pb_count // inner + inner * ka_count) * (1 + extra)
    return (
        selected.shape[0] == 1
        and extra > 0
        and block_rows == head_width == 128
        and tiles * tile_bytes < VMEM_BUDGET
    )


def either(*arrays):
    return kernel_shards(*arrays) if fits_kernel(*arrays) else shards(*arrays)


def solution(mesh):
    return jax.shard_map(
        either,
        mesh=mesh,
        in_specs=(
            P(("pb", "ka"), None),
            P(("pb", "ka"), None),
            P(("pb", "ka"), None),
            P(("pb", "ka"), None),
            P(("pb", "ka"), None),
            P(None, ("pb", "ka")),
            P(("pb", "ka"), None),
            P(("pb", "ka")),
        ),
        out_specs=(P(("pb", "ka"), None), P(("pb", "ka"), None), P(("pb", "ka"), None)),
        check_vma=False,
    )
```

```python
import functools

import jax
import jax.numpy as jnp
from jax import lax
from jax.experimental import pallas as pl
from jax.experimental.pallas import tpu as pltpu
from jax.sharding import PartitionSpec as P

VERY_LOW = -1e30


def passed_along(value, axis, steps):
    count = lax.axis_size(axis)
    pairs = [(source, (source + steps) % count) for source in range(count)]
    return lax.ppermute(value, axis, pairs)


def head_sums(grad_rows, out_rows, head_width):
    row_total = grad_rows.shape[0]
    part_heads = grad_rows.shape[1] // head_width
    product = grad_rows.astype(jnp.float32) * out_rows.astype(jnp.float32)
    return jnp.sum(product.reshape(row_total, part_heads, head_width), axis=2).T


def shards(query_rows, key_rows, value_rows, outputs, out_grads, log_totals, selected, counts):
    ka_count = lax.axis_size("ka")
    ka_index = lax.axis_index("ka")
    pb_index = lax.axis_index("pb")
    block_count = selected.shape[0]
    slot_count = selected.shape[1]
    head_width = key_rows.shape[1]
    block_rows = query_rows.shape[0] // block_count
    score_scale = head_width ** (-0.5)
    key_pairs = jnp.concatenate([key_rows, value_rows], 1)
    column_keys = lax.all_gather(key_pairs, "pb", axis=0, tiled=True)
    peer_slots, peer_counts = (
        lax.all_gather(selected, "ka", axis=0, tiled=True),
        lax.all_gather(counts, "ka", axis=0, tiled=True),
    )
    key_grads = jnp.zeros((column_keys.shape[0], 2 * head_width), jnp.float32)
    row_offsets = jnp.arange(block_rows, dtype=jnp.int32)
    flat_owner = jnp.repeat(jnp.arange(block_count, dtype=jnp.int32), slot_count)
    flat_slot = jnp.tile(jnp.arange(slot_count, dtype=jnp.int32), block_count)
    flat_places = jnp.arange(block_count * slot_count, dtype=jnp.int32)

    def visit_block(row_stack, query_grad, stat_stack, anchor, key_grads):
        held_query = row_stack[0]
        held_grad = row_stack[1]
        total_rows = stat_stack[0]
        delta_rows = head_sums(row_stack[1], row_stack[2], head_width)
        part_heads = total_rows.shape[0]
        held_slots = lax.dynamic_slice_in_dim(
            peer_slots, anchor * block_count, block_count, 0
        ).reshape(-1)
        held_counts = jnp.repeat(
            lax.dynamic_slice_in_dim(peer_counts, anchor * block_count, block_count, 0), slot_count
        )
        first_block = (pb_index * ka_count + anchor) * block_count
        wanted = (flat_slot < held_counts) & (held_slots // block_count % ka_count == ka_index)
        position = jnp.cumsum(wanted.astype(jnp.int32)) - 1
        placed = wanted[:, None] & (position[:, None] == flat_places[None, :])
        packed_ids = jnp.sum(jnp.where(placed, held_slots[:, None], 0), axis=0)
        packed_owner = jnp.sum(jnp.where(placed, flat_owner[:, None], 0), axis=0)
        live_tiles = jnp.sum(wanted.astype(jnp.int32))

        def one_tile(tile_index, loop_state):
            query_grad, key_grads = loop_state
            key_block = packed_ids[tile_index]
            owner_block = packed_owner[tile_index]
            key_start = (
                key_block // (block_count * ka_count) * block_count + key_block % block_count
            ) * block_rows
            pair_tile = lax.dynamic_slice_in_dim(column_keys, key_start, block_rows, 0)
            key_tile = pair_tile[:, :head_width]
            value_tile = pair_tile[:, head_width:]
            query_tile = held_query.reshape(block_rows, part_heads, head_width)
            grad_tile = held_grad.reshape(block_rows, part_heads, head_width)
            scores = (
                jnp.einsum("rhd,cd->hrc", query_tile, key_tile, preferred_element_type=jnp.float32)
                * score_scale
            )
            query_pos = (first_block + owner_block) * block_rows + row_offsets
            key_pos = key_block * block_rows + row_offsets
            allowed = key_pos[None, :] <= query_pos[:, None]
            probs_full = jnp.exp(
                jnp.where(allowed[None], scores - total_rows[:, :, None], VERY_LOW)
            )
            prob_grads = jnp.einsum(
                "rhd,cd->hrc", grad_tile, value_tile, preferred_element_type=jnp.float32
            )
            score_grads = probs_full * (prob_grads - delta_rows[:, :, None])
            rounded_probs = probs_full.astype(jnp.bfloat16)
            rounded_grads = score_grads.astype(jnp.bfloat16)
            value_part = jnp.einsum(
                "hrc,rhd->cd", rounded_probs, grad_tile, preferred_element_type=jnp.float32
            )
            key_part = (
                jnp.einsum(
                    "hrc,rhd->cd", rounded_grads, query_tile, preferred_element_type=jnp.float32
                )
                * score_scale
            )
            query_part = (
                jnp.einsum(
                    "hrc,cd->rhd", rounded_grads, key_tile, preferred_element_type=jnp.float32
                )
                * score_scale
            )
            old_query = query_grad
            query_grad = old_query + query_part.reshape(block_rows, -1)
            old_keys = lax.dynamic_slice_in_dim(key_grads, key_start, block_rows, 0)
            key_grads = lax.dynamic_update_slice_in_dim(
                key_grads, old_keys + jnp.concatenate([key_part, value_part], 1), key_start, 0
            )
            return (query_grad, key_grads)

        return lax.fori_loop(0, live_tiles, one_tile, (query_grad, key_grads))

    query_part = query_rows
    grad_zero = jnp.zeros(query_part.shape, jnp.float32)
    row_stack = jnp.stack([query_part, out_grads, outputs])
    query_grad = grad_zero
    stat_stack = log_totals[None]

    def forward_hop(hop_index, loop_state):
        row_stack, query_grad, stat_stack, key_grads = loop_state
        anchor = (ka_index - hop_index) % ka_count
        query_grad, key_grads = visit_block(row_stack, query_grad, stat_stack, anchor, key_grads)
        row_stack = passed_along(row_stack, "ka", 1)
        query_grad, stat_stack = passed_along((query_grad, stat_stack), "ka", 1)
        return (row_stack, query_grad, stat_stack, key_grads)

    row_stack, query_grad, stat_stack, key_grads = lax.fori_loop(
        0, ka_count - 1, forward_hop, (row_stack, query_grad, stat_stack, key_grads)
    )
    query_grad, key_grads = visit_block(
        row_stack, query_grad, stat_stack, (ka_index + 1) % ka_count, key_grads
    )
    query_grad = passed_along(query_grad, "ka", 1)
    owned_grads = lax.psum_scatter(key_grads, "pb", scatter_dimension=0, tiled=True)
    return (query_grad, owned_grads[:, :head_width], owned_grads[:, head_width:])


MESH = pl.DeviceIdType.MESH
VMEM_BUDGET = 40 << 20


def tile_weights(key_tile, value_tile, query_stack, grad_stack, total_row, delta_row, allowed, scale):
    nt = (((1,), (1,)), ((), ()))
    scores = lax.dot_general(key_tile, query_stack, nt, preferred_element_type=jnp.float32) * scale
    probs = jnp.exp(jnp.where(allowed, scores - total_row, VERY_LOW))
    prob_grads = lax.dot_general(value_tile, grad_stack, nt, preferred_element_type=jnp.float32)
    score_grads = probs * (prob_grads - delta_row)
    return probs.astype(jnp.bfloat16), score_grads.astype(jnp.bfloat16)


def query_share(score_grads, key_tile, scale):
    tn = (((0,), (0,)), ((), ()))
    return lax.dot_general(score_grads, key_tile, tn, preferred_element_type=jnp.float32) * scale


def whole_kernel(
    ka_count, inner, line_count, extra,
    query_hbm, key_hbm, value_hbm, out_hbm, grad_hbm, total_hbm, selected_hbm, counts_hbm,
    query_grad_ref, key_grad_ref, value_grad_ref,
    query_ref, out_ref, grad_ref, total_ref, selected_ref, counts_ref,
    key_plane, key_line, key_line_out, value_line, value_plane, value_plane_out,
    kgrad_plane, kgrad_line, kgrad_line_out, vgrad_line, vgrad_plane, vgrad_plane_out,
    plane_info, line_info, query_stack, grad_stack, query_acc, key_acc, value_acc,
    info_send_p, info_recv_p, info_send_l, info_recv_l,
    key_send_p, key_recv_p, key_send_l, key_recv_l,
    value_send_p, value_recv_p, value_send_l, value_recv_l,
    kgrad_send_p, kgrad_recv_p, kgrad_send_l, kgrad_recv_l,
    vgrad_send_p, vgrad_recv_p, vgrad_send_l, vgrad_recv_l,
    load_sem,
):
    bf, f32 = jnp.bfloat16, jnp.float32
    plane_count = inner * ka_count
    pb_index, ka_index = lax.axis_index("pb"), lax.axis_index("ka")
    line = lax.div(pb_index, inner)
    row = lax.rem(pb_index, inner)
    place = row * ka_count + ka_index
    block_rows, head_width = key_hbm.shape
    heads = total_hbm.shape[0]
    scale = head_width ** (-0.5)
    block = line * plane_count + place

    def partner(me, offset, count):
        if count & (count - 1):
            return lax.rem(me + offset, count)
        peer, bit = me, 1
        while bit < count:
            if offset & bit:
                peer = peer + bit - 2 * bit * lax.rem(lax.div(me, bit), 2)
            bit *= 2
        return peer

    def plane_peer(offset):
        peer = partner(place, offset, plane_count)
        return peer, (line * inner + lax.div(peer, ka_count), lax.rem(peer, ka_count))

    def line_peer(offset):
        peer = partner(line, offset, line_count)
        return peer, (peer * inner + row, ka_index)

    plane = (plane_peer, plane_count, place)
    column = (line_peer, line_count, line)

    barrier = pltpu.get_barrier_semaphore()
    for peer_of, count, _ in (plane, column):
        for offset in range(1, count):
            pl.semaphore_signal(barrier, inc=1, device_id=peer_of(offset)[1], device_id_type=MESH)
    loads = [
        pltpu.make_async_copy(source, target, load_sem.at[index])
        for index, (source, target) in enumerate((
            (selected_hbm, selected_ref), (counts_hbm, counts_ref),
            (key_hbm, key_plane.at[place]), (value_hbm, value_line.at[line]),
            (query_hbm, query_ref), (grad_hbm, grad_ref), (out_hbm, out_ref), (total_hbm, total_ref),
        ))
    ]
    for load in loads:
        load.start()

    loads[0].wait()
    loads[1].wait()
    targets = [
        jnp.where(slot + 1 < counts_ref[0], selected_ref[0, slot + 1], -1) for slot in range(extra)
    ]
    for slot in range(extra):
        lines = jnp.full((8, 128), targets[slot], jnp.int32)
        plane_info[place, slot] = lines
        line_info[line, slot] = lines

    sent = []

    def send(group, offset, source, target, send_sem, recv_sem):
        peer_of, _, me = group
        copy = pltpu.make_async_remote_copy(
            src_ref=source, dst_ref=target.at[me], send_sem=send_sem.at[offset],
            recv_sem=recv_sem.at[me], device_id=peer_of(offset)[1], device_id_type=MESH,
        )
        copy.start()
        sent.append(copy)

    def spread(group, target, send_sem, recv_sem):
        for offset in range(group[1] - 1, 0, -1):
            send(group, offset, target.at[group[2]], target, send_sem, recv_sem)

    def arrive(group, target, send_sem, recv_sem):
        peer_of, count, _ = group
        for offset in range(1, count):
            peer, device = peer_of(offset)
            pltpu.make_async_remote_copy(
                src_ref=target.at[peer], dst_ref=target.at[peer], send_sem=send_sem.at[offset],
                recv_sem=recv_sem.at[peer], device_id=device, device_id_type=MESH,
            ).wait_recv()

    loads[2].wait()
    loads[3].wait()
    pl.semaphore_wait(barrier, plane_count + line_count - 2)
    spread(column, line_info, info_send_l, info_recv_l)
    spread(plane, plane_info, info_send_p, info_recv_p)
    spread(column, value_line, value_send_l, value_recv_l)
    spread(plane, key_plane, key_send_p, key_recv_p)

    for load in loads[4:]:
        load.wait()
    deltas = []
    for head in range(heads):
        columns = pl.ds(head * head_width, head_width)
        rows = pl.ds(head * block_rows, block_rows)
        query_stack[rows, :] = query_ref[:, columns]
        grad_stack[rows, :] = grad_ref[:, columns]
        product = grad_ref[:, columns].astype(f32) * out_ref[:, columns].astype(f32)
        deltas.append(jnp.sum(product.T, axis=0, keepdims=True))
    delta_row = jnp.concatenate(deltas, axis=1)
    total_row = jnp.concatenate([total_ref[head : head + 1, :] for head in range(heads)], axis=1)
    stack_shape = (block_rows, heads * block_rows)
    key_offset = lax.broadcasted_iota(jnp.int32, stack_shape, 0)
    query_offset = lax.rem(lax.broadcasted_iota(jnp.int32, stack_shape, 1), block_rows)

    arrive(column, line_info, info_send_l, info_recv_l)
    arrive(plane, plane_info, info_send_p, info_recv_p)

    def pick(group, info, held, held_count, first, step, out, target, send_sem, recv_sem):
        peer_of, count, me = group
        for offset in range(count - 1, -1, -1):
            peer, _ = peer_of(offset)
            for slot in range(extra):
                wanted = info[peer, slot][0:1, :]
                picked = jnp.zeros(held.shape[1:], f32)
                for other in range(held_count):
                    picked = jnp.where(wanted == first + other * step, held[other].astype(f32), picked)
                if offset:
                    out[peer, slot] = picked.astype(bf)
                else:
                    target[me, slot] = picked.astype(bf)
            if offset:
                send(group, offset, out.at[peer], target, send_sem, recv_sem)

    arrive(column, value_line, value_send_l, value_recv_l)
    pick(plane, plane_info, value_line, line_count, place, plane_count,
         value_plane_out, value_plane, value_send_p, value_recv_p)
    arrive(plane, key_plane, key_send_p, key_recv_p)
    pick(column, line_info, key_plane, plane_count, line * plane_count, 1,
         key_line_out, key_line, key_send_l, key_recv_l)

    own_key = key_plane[place]
    probs, score_grads = tile_weights(
        own_key, value_line[line], query_stack[...], grad_stack[...], total_row, delta_row,
        key_offset <= query_offset, scale,
    )
    query_acc[...] = query_share(score_grads, own_key, scale)
    key_acc[...] = jnp.dot(score_grads, query_stack[...], preferred_element_type=f32) * scale
    value_acc[...] = jnp.dot(probs, grad_stack[...], preferred_element_type=f32)

    arrive(column, key_line, key_send_l, key_recv_l)
    arrive(plane, value_plane, value_send_p, value_recv_p)
    late = []
    for slot in range(extra):
        listed = jnp.maximum(targets[slot], 0)
        key_tile = key_line[lax.div(listed, plane_count), slot]
        value_tile = value_plane[lax.rem(listed, plane_count), slot]
        allowed = (key_offset + targets[slot] * block_rows <= query_offset + block * block_rows) & (
            jnp.full(stack_shape, targets[slot], jnp.int32) >= 0
        )
        probs, score_grads = tile_weights(
            key_tile, value_tile, query_stack[...], grad_stack[...], total_row, delta_row, allowed, scale
        )
        vgrad_line[line, slot] = jnp.dot(probs, grad_stack[...], preferred_element_type=f32).astype(bf)
        kgrad_plane[place, slot] = (
            jnp.dot(score_grads, query_stack[...], preferred_element_type=f32) * scale
        ).astype(bf)
        late.append((score_grads, key_tile))
    spread(column, vgrad_line, vgrad_send_l, vgrad_recv_l)
    spread(plane, kgrad_plane, kgrad_send_p, kgrad_recv_p)
    for score_grads, key_tile in late:
        query_acc[...] += query_share(score_grads, key_tile, scale)
    for head in range(heads):
        query_grad_ref[:, pl.ds(head * head_width, head_width)] = query_acc[
            pl.ds(head * block_rows, block_rows), :
        ]

    def combine(group, info, held, held_count, first, step, out, target, send_sem, recv_sem):
        peer_of, count, _ = group
        for offset in range(count - 1, -1, -1):
            peer, _ = peer_of(offset)
            sums = jnp.zeros(held.shape[2:], f32)
            for other in range(held_count):
                for slot in range(extra):
                    aimed = info[other, slot][0:1, :] == first + peer * step
                    sums = sums + jnp.where(aimed, held[other, slot].astype(f32), 0.0)
            if offset:
                out[peer] = sums.astype(bf)
                send(group, offset, out.at[peer], target, send_sem, recv_sem)
        return sums

    arrive(column, vgrad_line, vgrad_send_l, vgrad_recv_l)
    value_total = combine(plane, line_info, vgrad_line, line_count, line * plane_count, 1,
                          vgrad_plane_out, vgrad_plane, vgrad_send_p, vgrad_recv_p)
    arrive(plane, kgrad_plane, kgrad_send_p, kgrad_recv_p)
    key_total = combine(column, plane_info, kgrad_plane, plane_count, place, plane_count,
                        kgrad_line_out, kgrad_line, kgrad_send_l, kgrad_recv_l)
    value_total = value_total + value_acc[...]
    key_total = key_total + key_acc[...]
    arrive(column, kgrad_line, kgrad_send_l, kgrad_recv_l)
    for offset in range(1, line_count):
        key_total = key_total + kgrad_line[line_peer(offset)[0]].astype(f32)
    key_grad_ref[...] = key_total
    arrive(plane, vgrad_plane, vgrad_send_p, vgrad_recv_p)
    for offset in range(1, plane_count):
        value_total = value_total + vgrad_plane[plane_peer(offset)[0]].astype(f32)
    value_grad_ref[...] = value_total
    for copy in sent:
        copy.wait_send()


def kernel_shards(query_rows, key_rows, value_rows, outputs, out_grads, log_totals, selected, counts):
    ka_count, pb_count = lax.axis_size("ka"), lax.axis_size("pb")
    inner = 2 if pb_count % 2 == 0 else 1
    line_count, plane_count = pb_count // inner, inner * ka_count
    extra = selected.shape[1] - 1
    block_rows, head_width = key_rows.shape
    heads = log_totals.shape[0]
    tile = key_rows.shape
    dma = pltpu.SemaphoreType.DMA
    vmem = pl.BlockSpec(memory_space=pltpu.VMEM)
    hbm = pl.BlockSpec(memory_space=pl.ANY)
    bf, f32 = jnp.bfloat16, jnp.float32
    shapes = (query_rows.shape, key_rows.shape, value_rows.shape)
    held = pl.pallas_call(
        functools.partial(whole_kernel, ka_count, inner, line_count, extra),
        out_shape=tuple(pltpu.VMEM(shape, f32) for shape in shapes),
        in_specs=[hbm] * 8,
        out_specs=(vmem, vmem, vmem),
        scratch_shapes=[
            pltpu.VMEM(query_rows.shape, bf),
            pltpu.VMEM(query_rows.shape, bf),
            pltpu.VMEM(query_rows.shape, bf),
            pltpu.VMEM(log_totals.shape, f32),
            pltpu.SMEM(selected.shape, jnp.int32),
            pltpu.SMEM(counts.shape, jnp.int32),
            pltpu.VMEM((plane_count, *tile), bf),
            pltpu.VMEM((line_count, extra, *tile), bf),
            pltpu.VMEM((line_count, extra, *tile), bf),
            pltpu.VMEM((line_count, *tile), bf),
            pltpu.VMEM((plane_count, extra, *tile), bf),
            pltpu.VMEM((plane_count, extra, *tile), bf),
            pltpu.VMEM((plane_count, extra, *tile), bf),
            pltpu.VMEM((line_count, *tile), bf),
            pltpu.VMEM((line_count, *tile), bf),
            pltpu.VMEM((line_count, extra, *tile), bf),
            pltpu.VMEM((plane_count, *tile), bf),
            pltpu.VMEM((plane_count, *tile), bf),
            pltpu.VMEM((plane_count, extra, 8, 128), jnp.int32),
            pltpu.VMEM((line_count, extra, 8, 128), jnp.int32),
            pltpu.VMEM((heads * block_rows, head_width), bf),
            pltpu.VMEM((heads * block_rows, head_width), bf),
            pltpu.VMEM((heads * block_rows, head_width), f32),
            pltpu.VMEM(tile, f32),
            pltpu.VMEM(tile, f32),
            *[dma((count,)) for count in (plane_count, plane_count, line_count, line_count) * 5],
            dma((8,)),
        ],
        compiler_params=pltpu.CompilerParams(collective_id=0, has_side_effects=True),
    )(query_rows, key_rows, value_rows, outputs, out_grads, log_totals, selected, counts)
    return pl.pallas_call(
        write_kernel,
        out_shape=tuple(jax.ShapeDtypeStruct(shape, f32) for shape in shapes),
        in_specs=[vmem] * 3,
        out_specs=(hbm, hbm, hbm),
        scratch_shapes=[dma((3,))],
    )(*[pltpu.with_memory_space_constraint(part, pltpu.VMEM) for part in held])


def write_kernel(*refs):
    sources, targets, sem = refs[:3], refs[3:6], refs[6]
    stores = [pltpu.make_async_copy(*pair, sem.at[i]) for i, pair in enumerate(zip(sources, targets))]
    for store in stores:
        store.start()
    for store in stores:
        store.wait()


def fits_kernel(query_rows, key_rows, value_rows, outputs, out_grads, log_totals, selected, counts):
    pb_count, ka_count = lax.axis_size("pb"), lax.axis_size("ka")
    block_rows, head_width = key_rows.shape
    inner = 2 if pb_count % 2 == 0 else 1
    extra = selected.shape[1] - 1
    tile_bytes = 2 * block_rows * head_width
    tiles = 3 * (pb_count // inner + inner * ka_count) * (1 + extra)
    return (
        selected.shape[0] == 1
        and extra > 0
        and block_rows == head_width == 128
        and tiles * tile_bytes < VMEM_BUDGET
    )


def either(*arrays):
    return kernel_shards(*arrays) if fits_kernel(*arrays) else shards(*arrays)


def solution(mesh):
    return jax.shard_map(
        either,
        mesh=mesh,
        in_specs=(
            P(("pb", "ka"), None),
            P(("pb", "ka"), None),
            P(("pb", "ka"), None),
            P(("pb", "ka"), None),
            P(("pb", "ka"), None),
            P(None, ("pb", "ka")),
            P(("pb", "ka"), None),
            P(("pb", "ka")),
        ),
        out_specs=(P(("pb", "ka"), None), P(("pb", "ka"), None), P(("pb", "ka"), None)),
        check_vma=False,
    )
```
